128 devices in a mesh: azimuth: 16 (over y_hi, z, core), radius: 8 (over x, y_lo).
Axes of the slice: x: 4, y: 4 (y_hi: 2, y_lo: 2; y = y_hi * 2 + y_lo), z: 4, core: 2. Of those that a mesh axis runs over, the one named last changes fastest.
Arguments:
- flow_state: float32 [5, 256, 256, 384], P(None, 'azimuth', 'radius'), may hold values from -6 to 6
- base_state: float32 [5, 256, 256, 384], P(None, 'azimuth', 'radius'), may hold values from -6 to 6
- mean_flow: float32 [2, 256], P(None, 'radius'), may hold values from 0.1 to 0.5
- panel_history: bfloat16 [16, 8, 16, 2016], P('azimuth', 'radius'), may hold values from -6 to 6
- panel_line: int32 [16, 8, 16], P('azimuth', 'radius'), may hold values from 0 to 511
- panel_start: int32 [16, 8, 16], P('azimuth', 'radius'), may hold values from 0 to 352
- panel_count: int32 [16, 8], replicated, may hold values from 2 to 16, as said below
- panel_owner: int32 [16, 8, 16], replicated, may hold values from 0 to 15, as said below
- source_weight: bfloat16 [8, 16384, 4096], P('radius', 'azimuth'), may hold values from -0.046875 to 0.046875
- retarded_time: float32 [128, 64, 64], replicated, may hold values from -0.75 to 0.75
- observer_block: int32 [128], replicated, may hold values from 0 to 127, each once
Outputs:
- next_state: float32 [5, 256, 256, 384], P(None, 'azimuth', 'radius')
- observer_pressure: float32 [128, 2048], P(('azimuth', 'radius'))
The draws below stay inside these ranges and needn't reach their ends.
Inputs may be any that keep to these rules, and one draw needn't show every extreme that they name: The slots 0 to panel_count[a, b] - 1 of device (a, b) are live. `panel_owner`: entries of slots that are not live are ignored. At most 2 live blocks of one device go to one owner, and in every radius band some owner receives exactly 2 live blocks from every device of the band.
All inputs are finite; a program needn't handle non-finite values.
Results may differ from the reference program's by a relative error of at most 0.00039.
Values may be sent and summed in bfloat16 or wider, within the bound.
No kernel may reach another device: no remote copies, remote signals or barrier semaphores. Data moves between devices by JAX's collectives and lax.ppermute only.
A program may use at most 192 MiB of HBM per device.

```python
import math
import jax
import jax.numpy as jnp
from jax import lax

CA = 16
CR = 32
CZ = 384
NVAR = 5
NT = 64
BP = 32
KMAX = 16
CAP = 2
OBS = 4096
NA = 256
NR = 256
NOB = 128
OB = 32
STATIONS = 32
N_AZIMUTH = 16
N_RADIUS = 8


def route_tables(key):
    base_key = jax.random.fold_in(key, 41)
    band_keys = jax.random.split(base_key, N_RADIUS)

    def one_band(band_key):
        hot_key, count_key, turn_key = jax.random.split(band_key, 3)
        hottest = jax.random.randint(hot_key, (), 0, N_AZIMUTH, dtype=jnp.int32)
        counts = jax.random.randint(count_key, (N_AZIMUTH,), CAP, KMAX + 1, dtype=jnp.int32)
        shuffled = jax.random.permutation(turn_key, N_AZIMUTH - 1).astype(jnp.int32)
        slot_ids = jnp.arange(KMAX, dtype=jnp.int32)
        turns = shuffled[jnp.maximum(slot_ids - CAP, 0) % (N_AZIMUTH - 1)]
        sources = jnp.arange(N_AZIMUTH, dtype=jnp.int32)
        relative = (sources - hottest) % N_AZIMUTH
        spread = (relative[:, None] - 1 + turns[None, :]) % (N_AZIMUTH - 1)
        regular = (hottest + 1 + spread) % N_AZIMUTH
        owners = jnp.where(slot_ids[None, :] < CAP, hottest, regular).astype(jnp.int32)
        return (counts, owners)
    counts, owners = jax.vmap(one_band)(band_keys)
    return (jnp.transpose(counts), jnp.transpose(owners, (1, 0, 2)))


def draw_panel_count(key, part):
    return route_tables(key)[0]


def draw_panel_owner(key, part):
    return route_tables(key)[1]


def with_ends(drawn, own_key, low, high):
    longest = drawn.shape.index(max(drawn.shape))
    spots = []
    for shift in (0, 1):
        where = [jax.random.randint(jax.random.fold_in(own_key, axis), (), 0, length) for axis, length in enumerate(drawn.shape)]
        where[longest] = (where[longest] + shift) % drawn.shape[longest]
        spots.append(tuple(where))
    return drawn.at[spots[0]].set(low).at[spots[1]].set(high)


def with_spikes(entries, rng, source, target, blocks, factor):
    def block_of(dim):
        return (jnp.arange(entries.shape[dim]) // (entries.shape[dim] // blocks)).reshape((-1,) + (1,) * (entries.ndim - 1 - dim))

    one_side = jax.random.permutation(rng, blocks)[block_of(target)]
    second = (block_of(target) + blocks // 2) % blocks
    return jnp.where((block_of(source) == one_side) | (block_of(source) == second), factor * entries, entries)


def level_of(stream_key, dims, cuts, smallest, high):
    level, own = 1.0, jax.random.fold_in(stream_key, 6)
    for dim, shards_of in cuts:
        steps = jnp.exp(jax.random.uniform(jax.random.fold_in(own, dim), (shards_of,), jnp.float32, smallest / len(cuts), high / len(cuts)))
        level = level * jnp.repeat(steps, dims[dim] // shards_of).reshape([-1 if axis == dim else 1 for axis in range(len(dims))])
    return level


def centred(key, shape, scale, reach, cuts=(), held_as=jnp.bfloat16):
    factor_of = level_of(key, shape, cuts, -0.22, 0.18) if cuts else 1.0
    values = jax.random.normal(key, shape, jnp.float32) * scale * factor_of
    return jnp.minimum(jnp.maximum(values, -reach), reach).astype(held_as)


def gaussian_with(rng, shape, scale, limit, pieces, heavy, kind=jnp.bfloat16):
    values = scale * jax.random.normal(rng, shape, jnp.float32)
    if pieces:
        values = values * level_of(rng, shape, pieces, -0.22, 0.18)
    return jnp.clip(with_spikes(values, jax.random.fold_in(rng, 3), *heavy), -limit, limit).astype(kind)


def setup_inputs(seed: int = 0) -> dict:
    streams_of = jax.random.split(jax.random.key(seed), 12)
    return {
        "flow_state": centred(streams_of[0], (NVAR, NA, NR, CZ), 1.0, 6.0, ((1, 16), (2, 8)), jnp.float32),
        "base_state": centred(streams_of[1], (NVAR, NA, NR, CZ), 1.0, 6.0, ((1, 16), (2, 8)), jnp.float32),
        "mean_flow": jnp.clip(0.1 + 0.4 * jax.random.uniform(streams_of[2], (2, NR), jnp.float32) ** level_of(streams_of[2], (2, NR), ((1, 8),), -0.2, 0.2), 0.1, 0.5),
        "panel_history": centred(streams_of[3], (N_AZIMUTH, N_RADIUS, KMAX, (NT - 1) * BP), 1.0, 6.0, ((0, 16), (1, 8))),
        "panel_line": with_ends(jax.random.randint(streams_of[4], (N_AZIMUTH, N_RADIUS, KMAX), 0, CA * CR), jax.random.fold_in(streams_of[4], 1), 0, (CA * CR) - 1).astype(jnp.int32),
        "panel_start": with_ends(jax.random.randint(streams_of[5], (N_AZIMUTH, N_RADIUS, KMAX), 0, CZ - BP + 1), jax.random.fold_in(streams_of[5], 1), 0, CZ - BP).astype(jnp.int32),
        "panel_count": draw_panel_count(jax.random.fold_in(streams_of[11], 71), 0),
        "panel_owner": draw_panel_owner(jax.random.fold_in(streams_of[11], 71), 0),
        "source_weight": gaussian_with(streams_of[8], (N_RADIUS, N_AZIMUTH * STATIONS * BP, OBS), (N_RADIUS * N_AZIMUTH * (CAP + KMAX) * BP // 2) ** -0.5, 0.046875, ((0, 8), (1, 16)), (1, 2, 16, 2.0)),
        "retarded_time": centred(streams_of[9], (NOB, NT, NT), NT ** -0.5, 0.75, (), jnp.float32),
        "observer_block": jax.random.permutation(streams_of[10], NOB).astype(jnp.int32),
    }


SECTION_STEP = 0.3
VISCOSITY = 0.05


def first_diff(extended, axis_dim, length):
    def shifted(offset):
        return lax.slice_in_dim(extended, 2 + offset, 2 + offset + length, axis=axis_dim)
    return (8.0 * (shifted(1) - shifted(-1)) - (shifted(2) - shifted(-2))) / 12.0


def second_diff(extended, axis_dim, length):
    def shifted(offset):
        return lax.slice_in_dim(extended, 2 + offset, 2 + offset + length, axis=axis_dim)
    return (16.0 * (shifted(1) + shifted(-1)) - (shifted(2) + shifted(-2)) - 30.0 * shifted(0)) / 12.0


def tendency(fields, cycle_ext, band_ext, mean_flow, radius_pos, arc_factor):
    cycle_length = fields.shape[1]
    band_length = fields.shape[2]
    axial_length = fields.shape[3]
    axial_ext = jnp.pad(fields, ((0, 0), (0, 0), (0, 0), (2, 2)))
    cycle_diff = first_diff(cycle_ext, 1, cycle_length)
    band_diff = first_diff(band_ext, 2, band_length)
    axial_diff = first_diff(axial_ext, 3, axial_length)
    smoothing = second_diff(cycle_ext, 1, cycle_length) + second_diff(band_ext, 2, band_length) + second_diff(axial_ext, 3, axial_length)
    swirl_flow = mean_flow[0][:, None]
    axial_flow = mean_flow[1][:, None]
    metric = arc_factor[:, None]
    inverse = 1.0 / radius_pos[:, None]
    carried = swirl_flow * metric * cycle_diff + axial_flow * axial_diff
    spread = metric * cycle_diff[1] + band_diff[2] + fields[2] * inverse + axial_diff[3]
    forcing = jnp.stack([spread, metric * cycle_diff[4], band_diff[4], axial_diff[4], spread])
    return VISCOSITY * smoothing - carried - forcing


def reference(flow_state, base_state, mean_flow, panel_history, panel_line, panel_start, panel_count, panel_owner, source_weight, retarded_time, observer_block):
    cycle_ext = jnp.concatenate([flow_state[:, -2:], flow_state, flow_state[:, :2]], axis=1)
    band_ext = jnp.pad(flow_state, ((0, 0), (0, 0), (2, 2), (0, 0)))
    radius_pos = jnp.arange(NR, dtype=jnp.int32).astype(jnp.float32) + (0.5 * NR + 0.5)
    arc_factor = (NA / (2.0 * math.pi)) / radius_pos
    next_state = base_state + SECTION_STEP * tendency(flow_state, cycle_ext, band_ext, mean_flow, radius_pos, arc_factor)

    pressure_field = next_state[4]
    cycle_rows = (jnp.arange(N_AZIMUTH, dtype=jnp.int32) * CA)[:, None, None] + panel_line // CR
    band_rows = (jnp.arange(N_RADIUS, dtype=jnp.int32) * CR)[None, :, None] + panel_line % CR

    def cut_window(cycle_row, band_row, start_index):
        return lax.dynamic_slice(pressure_field, (cycle_row, band_row, start_index), (1, 1, BP)).reshape(BP)

    fresh_panels = jax.vmap(cut_window)(cycle_rows.reshape(-1).astype(jnp.int32), band_rows.reshape(-1).astype(jnp.int32), panel_start.reshape(-1).astype(jnp.int32))
    fresh_panels = fresh_panels.reshape(N_AZIMUTH, N_RADIUS, KMAX, BP)
    blocks = jnp.concatenate([panel_history, fresh_panels.astype(jnp.bfloat16)], axis=3)

    slot_ids = jnp.arange(KMAX, dtype=jnp.int32)
    alive_slots = slot_ids < panel_count[..., None]
    earlier = slot_ids[:, None] < slot_ids[None, :]
    matches = (panel_owner[..., :, None] == panel_owner[..., None, :]) & alive_slots[..., :, None] & earlier
    ranking = jnp.sum(matches.astype(jnp.int32), axis=-2)
    slot_places = jnp.arange(CAP, dtype=jnp.int32)
    station_rows = STATIONS * BP
    zero_index = jnp.zeros((), jnp.int32)

    def owner_term(running, flat_index):
        band_id = (flat_index // N_AZIMUTH).astype(jnp.int32)
        owner_id = (flat_index % N_AZIMUTH).astype(jnp.int32)
        band_blocks = lax.dynamic_index_in_dim(blocks, band_id, 1, keepdims=False)
        band_owner = lax.dynamic_index_in_dim(panel_owner, band_id, 1, keepdims=False)
        band_alive = lax.dynamic_index_in_dim(alive_slots, band_id, 1, keepdims=False)
        band_rank = lax.dynamic_index_in_dim(ranking, band_id, 1, keepdims=False)
        selection = band_alive[:, None, :] & (band_owner[:, None, :] == owner_id) & (band_rank[:, None, :] == slot_places[None, :, None])
        stations = jnp.einsum("dck,dkf->dcf", selection.astype(jnp.float32), band_blocks.astype(jnp.float32))
        weights = lax.dynamic_slice(source_weight, (band_id, owner_id * station_rows, zero_index), (1, station_rows, OBS))[0]
        term = jnp.einsum("stp,spo->to", stations.reshape(STATIONS, NT, BP), weights.astype(jnp.float32).reshape(STATIONS, BP, OBS))
        return running + term, None

    partial_value, unused = lax.scan(owner_term, jnp.zeros((NT, OBS), jnp.float32), jnp.arange(N_RADIUS * N_AZIMUTH, dtype=jnp.int32))
    grouped = partial_value.reshape(NT, NOB, OB)
    ordered = jnp.take(grouped, observer_block, axis=1)
    matrices = jnp.take(retarded_time, observer_block, axis=0)
    pressure = jnp.einsum("its,sio->ito", matrices, ordered, precision=lax.Precision.HIGHEST)
    return next_state, pressure.reshape(NOB, NT * OB)
```

```python
import functools
import math

import jax
import jax.numpy as jnp
from jax import lax
from jax.experimental import pallas as pl
from jax.experimental.pallas import tpu as pltpu
from jax.sharding import PartitionSpec as P

NT = 64
BP = 32
KMAX = 16
CAP = 2
LANES = 128
ROWS = NT * BP // LANES
QUADS = LANES // BP

SECTION_STEP = 0.3
VISCOSITY = 0.05
BOTH = ("azimuth", "radius")

FIRST_AZ = (1, 4)
FIRST_RAD = (2, 4)
LATER_AZ = (0, 2, 3)
LATER_RAD = (0, 1, 3)


def swap_quads(tiles):
    lane = lax.broadcasted_iota(jnp.int32, tiles[0].shape, 1)
    low, even = (lane % 128) < 64, (lane % 64) < 32
    a0, a1, a2, a3 = tiles

    def turn(x, shift):
        return pltpu.roll(x, shift, 1)

    b0 = jnp.where(low, a0, turn(a2, 64))
    b2 = jnp.where(low, turn(a0, 64), a2)
    b1 = jnp.where(low, a1, turn(a3, 64))
    b3 = jnp.where(low, turn(a1, 64), a3)
    return (
        jnp.where(even, b0, turn(b1, 32)),
        jnp.where(even, turn(b0, 96), b1),
        jnp.where(even, b2, turn(b3, 32)),
        jnp.where(even, turn(b2, 96), b3),
    )


def wide(tile, length):
    return jnp.concatenate([tile] * (length // tile.shape[1]), axis=1)


def tall(tile, length):
    return jnp.concatenate([tile] * (length // tile.shape[0]), axis=0)


def radial_shifts(x, lo, hi):
    n = x.shape[0]
    row = lax.broadcasted_iota(jnp.int32, (8, x.shape[1]), 0)
    m1, m2 = pltpu.roll(x, 1, 0), pltpu.roll(x, 2, 0)
    p1, p2 = pltpu.roll(x, n - 1, 0), pltpu.roll(x, n - 2, 0)
    m1 = jnp.concatenate([jnp.where(row == 0, lo[1], m1[:8]), m1[8:]], axis=0)
    m2 = jnp.concatenate(
        [jnp.where(row == 0, lo[0], jnp.where(row == 1, lo[1], m2[:8])), m2[8:]], axis=0
    )
    p1 = jnp.concatenate([p1[:-8], jnp.where(row == 7, hi[0], p1[-8:])], axis=0)
    p2 = jnp.concatenate(
        [p2[:-8], jnp.where(row == 6, hi[0], jnp.where(row == 7, hi[1], p2[-8:]))], axis=0
    )
    return p1, m1, p2, m2


def axial_shifts(x):
    n = x.shape[1]
    return (
        pltpu.roll(x, n - 1, 1),
        pltpu.roll(x, 1, 1),
        pltpu.roll(x, n - 2, 1),
        pltpu.roll(x, 2, 1),
    )


def new_plane(var, base, plane, layers, coef, axial_coef, edge_coef):
    rows, length = base.shape
    k8, k1 = SECTION_STEP * 8.0 / 12.0, SECTION_STEP / 12.0

    def row_coef(i):
        return wide(coef[i], length)

    def edge(i):
        return tall(edge_coef[i], rows)

    x = plane(var, 0)
    rp1, rm1, rp2, rm2 = radial_shifts(x, *layers(var))
    zp1, zm1, zp2, zm2 = axial_shifts(x)
    total = base + (-3.0 * 30.0 / 12.0 * SECTION_STEP * VISCOSITY) * x
    total += row_coef(0) * plane(var, 1) + row_coef(1) * plane(var, -1)
    total += row_coef(2) * plane(var, 2) + row_coef(3) * plane(var, -2)
    total += axial_coef[0] * zp1 + axial_coef[1] * zm1
    total += axial_coef[2] * zp2 + axial_coef[3] * zm2
    total += (SECTION_STEP * VISCOSITY * 16.0 / 12.0) * (rp1 + rm1)
    total -= (SECTION_STEP * VISCOSITY / 12.0) * (rp2 + rm2)
    if var in (0, 4):
        total -= row_coef(4) * (plane(1, 1) - plane(1, -1)) - row_coef(5) * (
            plane(1, 2) - plane(1, -2)
        )
        u = plane(2, 0)
        sp1, sm1, sp2, sm2 = radial_shifts(u, *layers(2))
        total -= k8 * (sp1 - sm1) - k1 * (sp2 - sm2) + row_coef(6) * u
        wp1, wm1, wp2, wm2 = axial_shifts(plane(3, 0))
        total -= edge(0) * wp1 - edge(1) * wm1 - edge(2) * wp2 + edge(3) * wm2
    elif var == 1:
        total -= row_coef(4) * (plane(4, 1) - plane(4, -1)) - row_coef(5) * (
            plane(4, 2) - plane(4, -2)
        )
    elif var == 2:
        sp1, sm1, sp2, sm2 = radial_shifts(plane(4, 0), *layers(4))
        total -= k8 * (sp1 - sm1) - k1 * (sp2 - sm2)
    else:
        wp1, wm1, wp2, wm2 = axial_shifts(plane(4, 0))
        total -= edge(0) * wp1 - edge(1) * wm1 - edge(2) * wp2 + edge(3) * wm2
    return total


def plane_copies(flow_ref, before_ref, after_ref, ext_ref, sems, variables, planes):
    def copies(spot):
        out = []
        for slot, (var, halo_slot, halo) in enumerate(variables):
            if isinstance(spot, int) and spot < 2:
                src = before_ref[halo].at[halo_slot, spot]
            elif isinstance(spot, int) and spot >= planes + 2:
                src = after_ref[halo].at[halo_slot, spot - planes - 2]
            else:
                src = flow_ref.at[var, spot - 2]
            out.append(pltpu.make_async_copy(src, ext_ref.at[slot, spot], sems.at[slot, spot]))
        return out

    return copies


def feed_planes(a, planes, copies):
    @pl.when(a == 0)
    def _():
        for spot in (0, 1):
            for c in copies(spot):
                c.start()
        for spot in range(2, planes + 2):
            for c in copies(spot):
                c.start()
        for spot in (planes + 2, planes + 3):
            for c in copies(spot):
                c.start()
        for spot in range(4):
            for c in copies(spot):
                c.wait()

    @pl.when(a + 4 < planes + 2)
    def _():
        for c in copies(a + 4):
            c.wait()

    for spot in (planes + 2, planes + 3):

        @pl.when(a + 4 == spot)
        def _():
            for c in copies(spot):
                c.wait()


def pressure_kernel(
    meta_ref,
    flow_ref,
    before_ref,
    after_ref,
    ur_ref,
    uz_ref,
    base_ref,
    lo_ref,
    hi_ref,
    coef_ref,
    axial_ref,
    edge_ref,
    history_ref,
    next_ref,
    out_ref,
    ext_ref,
    field_ref,
    wide_ref,
    block_ref,
    rank_ref,
    sems,
):
    a = pl.program_id(0)
    planes = pl.num_programs(0)
    n = field_ref.shape[0]
    variables = [(var, slot, 0) for slot, var in enumerate(FIRST_AZ)]
    copies = plane_copies(flow_ref, (before_ref,), (after_ref,), ext_ref, sems, variables, n)
    feed_planes(a, n, copies)

    def plane(var, offset):
        if var in FIRST_AZ:
            return ext_ref[FIRST_AZ.index(var), a + 2 + offset]
        return (ur_ref if var == 2 else uz_ref)[0, 0]

    def layers(var):
        s = FIRST_RAD.index(var)
        return (
            [lo_ref[s, a, j : j + 1, :] for j in (0, 1)],
            [hi_ref[s, a, j : j + 1, :] for j in (0, 1)],
        )

    value = new_plane(4, base_ref[0, 0], plane, layers, coef_ref, axial_ref, edge_ref)
    next_ref[0, 0] = value
    tiles = field_ref.shape[1]
    for t in range(tiles):
        field_ref[a, t] = value[:, t * LANES : (t + 1) * LANES]

    @pl.when(a == planes - 1)
    def _():
        band = field_ref.shape[2]
        for r in range(ROWS):
            width = min(LANES, history_ref.shape[1] - r * LANES)
            chunk = history_ref[:, r * LANES : r * LANES + width]
            wide_ref[r, :, 0:width] = chunk.astype(jnp.float32)
        out_ref[...] = jnp.zeros_like(out_ref)
        owners = out_ref.shape[0]
        for q in range(owners):
            rank_ref[q] = 0
        lane = lax.broadcasted_iota(jnp.int32, (1, LANES), 1)

        def one(k, carry):
            @pl.when(k < meta_ref[3 * KMAX])
            def _():
                owner = meta_ref[k]
                line = meta_ref[KMAX + k]
                start = meta_ref[2 * KMAX + k]
                rank = rank_ref[owner]
                rank_ref[owner] = rank + 1
                for r in range(ROWS):
                    block_ref[r : r + 1, :] = wide_ref[r, pl.ds(k, 1), :]
                tile = start // LANES
                off = start % LANES
                other = jnp.minimum(tile + 1, tiles - 1)
                at = pl.ds(line % band, 1)
                x0 = field_ref[line // band, tile, at, :]
                x1 = field_ref[line // band, other, at, :]
                shift = (2 * LANES - BP - off) % LANES
                r0 = pltpu.roll(jnp.broadcast_to(x0, (8, LANES)), shift, 1)[0:1]
                r1 = pltpu.roll(jnp.broadcast_to(x1, (8, LANES)), shift, 1)[0:1]
                window = jnp.where(lane < 2 * LANES - BP - off, r0, r1)
                last = block_ref[ROWS - 1 : ROWS, :]
                block_ref[ROWS - 1 : ROWS, :] = jnp.where(lane >= LANES - BP, window, last)
                out_ref[owner, pl.ds(pl.multiple_of(rank * ROWS, ROWS), ROWS), :] = block_ref[
                    ...
                ].astype(out_ref.dtype)

            return carry

        lax.fori_loop(0, KMAX, one, 0)


def rest_kernel(
    flow_ref,
    before0_ref,
    after0_ref,
    before1_ref,
    after1_ref,
    base_ref,
    lo0_ref,
    hi0_ref,
    lo1_ref,
    hi1_ref,
    coef_ref,
    axial_ref,
    edge_ref,
    held_ref,
    next_ref,
    ext_ref,
    sems,
):
    del held_ref
    a = pl.program_id(0)
    n = flow_ref.shape[1]
    variables = []
    for var in range(5):
        group = 0 if var in FIRST_AZ else 1
        variables.append((var, (FIRST_AZ, LATER_AZ)[group].index(var), group))
    copies = plane_copies(
        flow_ref, (before0_ref, before1_ref), (after0_ref, after1_ref), ext_ref, sems, variables, n
    )
    feed_planes(a, n, copies)

    def plane(var, offset):
        return ext_ref[var, a + 2 + offset]

    def layers(var):
        if var in FIRST_RAD:
            lo, hi, s = lo0_ref, hi0_ref, FIRST_RAD.index(var)
        else:
            lo, hi, s = lo1_ref, hi1_ref, LATER_RAD.index(var)
        return (
            [lo[s, a, j : j + 1, :] for j in (0, 1)],
            [hi[s, a, j : j + 1, :] for j in (0, 1)],
        )

    for var in range(4):
        next_ref[var, 0] = new_plane(
            var, base_ref[var, 0], plane, layers, coef_ref, axial_ref, edge_ref
        )


def whole(array):
    shape = array.shape
    return pl.BlockSpec(shape, lambda *_: (0,) * len(shape))


def pressure_call(meta, flow, before, after, base, lo, hi, coef, axial, edge, history, owners):
    nvar, planes, rows, length = flow.shape
    one = (1, 1, rows, length)
    any_space = pl.BlockSpec(memory_space=pl.ANY)
    cells = planes * rows * length
    return pl.pallas_call(
        pressure_kernel,
        name="pressure",
        out_shape=(
            jax.ShapeDtypeStruct(flow.shape, jnp.float32),
            jax.ShapeDtypeStruct((owners, CAP * ROWS, LANES), jnp.bfloat16),
        ),
        grid_spec=pltpu.PrefetchScalarGridSpec(
            num_scalar_prefetch=1,
            grid=(planes,),
            in_specs=[
                any_space,
                any_space,
                any_space,
                pl.BlockSpec(one, lambda a, m: (2, a, 0, 0)),
                pl.BlockSpec(one, lambda a, m: (3, a, 0, 0)),
                pl.BlockSpec(one, lambda a, m: (4, a, 0, 0)),
                whole(lo),
                whole(hi),
                whole(coef),
                whole(axial),
                whole(edge),
                whole(history),
            ],
            out_specs=(
                pl.BlockSpec(one, lambda a, m: (4, a, 0, 0)),
                pl.BlockSpec((owners, CAP * ROWS, LANES), lambda a, m: (0, 0, 0)),
            ),
            scratch_shapes=[
                pltpu.VMEM((2, planes + 4, rows, length), jnp.float32),
                pltpu.VMEM((planes, length // LANES, rows, LANES), jnp.float32),
                pltpu.VMEM((ROWS, KMAX, LANES), jnp.float32),
                pltpu.VMEM((ROWS, LANES), jnp.float32),
                pltpu.SMEM((owners,), jnp.int32),
                pltpu.SemaphoreType.DMA((2, planes + 4)),
            ],
        ),
        compiler_params=pltpu.CompilerParams(dimension_semantics=("arbitrary",)),
        cost_estimate=pl.CostEstimate(flops=60 * cells, bytes_accessed=6 * 4 * cells, transcendentals=0),
    )(meta, flow, before, after, flow, flow, base, lo, hi, coef, axial, edge, history)


def rest_call(flow, az0, az1, base, rad0, rad1, coef, axial, edge, held):
    nvar, planes, rows, length = flow.shape
    any_space = pl.BlockSpec(memory_space=pl.ANY)
    cells = planes * rows * length
    four = (4, 1, rows, length)
    args = (flow, *az0, *az1, base, *rad0, *rad1, coef, axial, edge, held)
    return pl.pallas_call(
        rest_kernel,
        name="others",
        out_shape=jax.ShapeDtypeStruct(flow.shape, jnp.float32),
        grid=(planes,),
        in_specs=[
            any_space,
            any_space,
            any_space,
            any_space,
            any_space,
            pl.BlockSpec(four, lambda a: (0, a, 0, 0)),
            *[whole(x) for x in (*rad0, *rad1, coef, axial, edge)],
            any_space,
        ],
        out_specs=pl.BlockSpec(four, lambda a: (0, a, 0, 0)),
        scratch_shapes=[
            pltpu.VMEM((nvar, planes + 4, rows, length), jnp.float32),
            pltpu.SemaphoreType.DMA((nvar, planes + 4)),
        ],
        input_output_aliases={len(args) - 1: 0},
        compiler_params=pltpu.CompilerParams(dimension_semantics=("arbitrary",)),
        cost_estimate=pl.CostEstimate(
            flops=200 * cells, bytes_accessed=13 * 4 * cells, transcendentals=0
        ),
    )(*args)


def weights_kernel(order_ref, stations_ref, weight_ref, out_ref, lhs_ref, packed_ref):
    step = pl.program_id(0)

    @pl.when(step == 0)
    def _():
        for group in range(stations_ref.shape[0] * CAP // QUADS):
            tiles = []
            for m in range(QUADS):
                source, rank = divmod(group * QUADS + m, CAP)
                tile = stations_ref[source, rank * ROWS : (rank + 1) * ROWS, :]
                tiles.append(tile.astype(jnp.float32))
            for i, tile in enumerate(swap_quads(tiles)):
                lhs_ref[i * ROWS : (i + 1) * ROWS, group * LANES : (group + 1) * LANES] = (
                    tile.astype(lhs_ref.dtype)
                )

    part = jnp.dot(lhs_ref[...], weight_ref[...], preferred_element_type=jnp.float32)
    groups = part.shape[1] // LANES
    for group in range(groups):
        lanes = slice(group * LANES, (group + 1) * LANES)
        tiles = [part[i * ROWS : (i + 1) * ROWS, lanes] for i in range(QUADS)]
        for m, tile in enumerate(swap_quads(tiles)):
            packed_ref[(step * groups + group) * QUADS + m] = tile

    @pl.when(step == pl.num_programs(0) - 1)
    def _():
        def move(j, carry):
            out_ref[j] = packed_ref[order_ref[j]]
            return carry

        lax.fori_loop(0, out_ref.shape[0], move, 0, unroll=8)


def weights_call(order, stations, weight):
    count = order.shape[0]
    depth, observers = weight.shape
    tile = 512
    return pl.pallas_call(
        weights_kernel,
        name="observers",
        out_shape=jax.ShapeDtypeStruct((count, ROWS, LANES), jnp.float32),
        grid_spec=pltpu.PrefetchScalarGridSpec(
            num_scalar_prefetch=1,
            grid=(observers // tile,),
            in_specs=[
                pl.BlockSpec(stations.shape, lambda n, o: (0, 0, 0)),
                pl.BlockSpec((depth, tile), lambda n, o: (0, n)),
            ],
            out_specs=pl.BlockSpec((count, ROWS, LANES), lambda n, o: (0, 0, 0)),
            scratch_shapes=[
                pltpu.VMEM((NT, depth), jnp.bfloat16),
                pltpu.VMEM((count, ROWS, LANES), jnp.float32),
            ],
        ),
        compiler_params=pltpu.CompilerParams(dimension_semantics=("arbitrary",)),
        cost_estimate=pl.CostEstimate(
            flops=2 * NT * depth * observers,
            bytes_accessed=2 * depth * observers,
            transcendentals=0,
        ),
    )(order, stations, weight)


def retard_kernel(parts_ref, matrix_ref, out_ref):
    def add(i, total):
        for j in range(8):
            total = total + parts_ref[i * 8 + j]
        return total

    total = lax.fori_loop(
        0, parts_ref.shape[0] // 8, add, jnp.zeros(parts_ref.shape[1:], jnp.float32)
    )
    tall_sum = jnp.concatenate(
        [total if i == 0 else pltpu.roll(total, LANES - i * BP, 1) for i in range(QUADS)], axis=0
    )
    pressure = jnp.dot(
        matrix_ref[...],
        tall_sum,
        precision=lax.Precision.HIGHEST,
        preferred_element_type=jnp.float32,
    )
    lane = lax.broadcasted_iota(jnp.int32, (ROWS, LANES), 1)
    out = pressure[:ROWS]
    for i in range(1, QUADS):
        tile = pltpu.roll(pressure[i * ROWS : (i + 1) * ROWS], i * BP, 1)
        out = jnp.where(lane >= i * BP, tile, out)
    out_ref[...] = out


def retard_call(parts, matrix):
    return pl.pallas_call(
        retard_kernel,
        name="retard",
        out_shape=jax.ShapeDtypeStruct((ROWS, LANES), jnp.float32),
        in_specs=[pl.BlockSpec(memory_space=pltpu.VMEM)] * 2,
        out_specs=pl.BlockSpec(memory_space=pltpu.VMEM),
        cost_estimate=pl.CostEstimate(
            flops=2 * parts.size, bytes_accessed=4 * parts.size, transcendentals=0
        ),
    )(parts, matrix)


def exchange(first, last, axis, wrap):
    count = lax.axis_size(axis)
    up = [(i, (i + 1) % count) for i in range(count if wrap else count - 1)]
    down = [(j, i) for i, j in up]
    return lax.ppermute(last, axis, up), lax.ppermute(first, axis, down)


def azimuth_layers(flow, variables):
    pick = lambda cut: jnp.stack([flow[v, cut] for v in variables])
    return exchange(pick(slice(0, 2)), pick(slice(-2, None)), "azimuth", True)


def radial_layers(flow, variables):
    def pick(cut):
        return jnp.stack([flow[v, :, cut] for v in variables])

    return exchange(pick(slice(0, 2)), pick(slice(-2, None)), "radius", False)


def coefficients(mean_flow, band_index, band_size, cycle_size, planes, rows, length):
    radial_cell = band_index * rows + jnp.arange(rows, dtype=jnp.int32)
    radius_pos = radial_cell.astype(jnp.float32) + (0.5 * rows * band_size + 0.5)
    metric = planes * cycle_size / (2.0 * math.pi) / radius_pos
    dt, nu = SECTION_STEP, VISCOSITY
    turn = mean_flow[0] * metric

    def four(speed):
        return [
            dt * (nu * 16.0 / 12.0 - speed * (8.0 / 12.0)),
            dt * (nu * 16.0 / 12.0 + speed * (8.0 / 12.0)),
            dt * (speed / 12.0 - nu / 12.0),
            -dt * (speed / 12.0 + nu / 12.0),
        ]

    coef = jnp.stack(
        four(turn) + [dt * 8.0 / 12.0 * metric, dt / 12.0 * metric, dt / radius_pos]
    )
    coef = jnp.broadcast_to(coef[:, :, None], (7, rows, LANES))
    z = jnp.arange(length, dtype=jnp.int32)
    inside = jnp.stack([z < length - 1, z >= 1, z < length - 2, z >= 2])
    axial = jnp.where(inside[:, None, :], jnp.stack(four(mean_flow[1]))[:, :, None], 0.0)
    scale = jnp.array([8.0 / 12.0, 8.0 / 12.0, 1.0 / 12.0, 1.0 / 12.0], jnp.float32) * dt
    edge = jnp.where(inside, scale[:, None], 0.0)
    edge = jnp.broadcast_to(edge[:, None, :], (4, 8, length))
    return coef, axial, edge


def per_device(
    flow_state,
    base_state,
    mean_flow,
    panel_history,
    panel_line,
    panel_start,
    panel_count,
    panel_owner,
    source_weight,
    retarded_time,
    observer_block,
):
    cycle_size = lax.axis_size("azimuth")
    band_size = lax.axis_size("radius")
    nvar, planes, rows, length = flow_state.shape
    cycle_index = lax.axis_index("azimuth")
    band_index = lax.axis_index("radius")

    rad0 = radial_layers(flow_state, FIRST_RAD)
    az0 = azimuth_layers(flow_state, FIRST_AZ)
    rad1 = radial_layers(flow_state, LATER_RAD)
    az1 = azimuth_layers(flow_state, LATER_AZ)
    coef, axial, edge = coefficients(
        mean_flow, band_index, band_size, cycle_size, planes, rows, length
    )
    own_owner = lax.dynamic_slice(panel_owner, (cycle_index, band_index, 0), (1, 1, KMAX))[0, 0]
    own_count = lax.dynamic_slice(panel_count, (cycle_index, band_index), (1, 1))[0]
    meta = jnp.concatenate([own_owner, panel_line[0, 0], panel_start[0, 0], own_count])

    held, outgoing = pressure_call(
        meta, flow_state, *az0, base_state, *rad0, coef, axial, edge, panel_history[0, 0], cycle_size
    )
    stations = lax.all_to_all(outgoing, "azimuth", split_axis=0, concat_axis=0, tiled=True)
    sends = weights_call(observer_block, stations, source_weight[0])
    parts = lax.all_to_all(sends, BOTH, split_axis=0, concat_axis=0, tiled=True)
    next_state = rest_call(
        flow_state, az0, az1, base_state, rad0, rad1, coef, axial, edge, held
    )

    chosen = lax.dynamic_index_in_dim(observer_block, lax.axis_index(BOTH), 0, keepdims=False)
    matrix = lax.dynamic_index_in_dim(retarded_time, chosen, 0, keepdims=False)
    matrix = matrix.reshape(ROWS, QUADS, ROWS, QUADS).transpose(1, 0, 3, 2).reshape(NT, NT)
    pressure = retard_call(parts, matrix)
    return next_state, pressure.reshape(1, ROWS * LANES)


def solution(mesh):
    placed = (
        P(None, "azimuth", "radius", None),
        P(None, "azimuth", "radius", None),
        P(None, "radius"),
        P("azimuth", "radius", None, None),
        P("azimuth", "radius", None),
        P("azimuth", "radius", None),
        P(),
        P(),
        P("radius", "azimuth", None),
        P(),
        P(),
    )
    return jax.shard_map(
        per_device,
        mesh=mesh,
        in_specs=placed,
        out_specs=(P(None, "azimuth", "radius", None), P(BOTH, None)),
        check_vma=False,
    )
```

```python
import functools
import math

import jax
import jax.numpy as jnp
from jax import lax
from jax.experimental import pallas as pl
from jax.experimental.pallas import tpu as pltpu
from jax.sharding import PartitionSpec as P

NT = 64
BP = 32
KMAX = 16
CAP = 2
LANES = 128
ROWS = NT * BP // LANES
QUADS = LANES // BP

SECTION_STEP = 0.3
VISCOSITY = 0.05
BOTH = ("azimuth", "radius")

NVAR = 5
FIRST_AZ = (1, 4)
FIRST_RAD = (2, 4)
LATER_AZ = (0, 2, 3)
LATER_RAD = (0, 1, 3)


def swap_quads(tiles):
    lane = lax.broadcasted_iota(jnp.int32, tiles[0].shape, 1)
    low, even = (lane % 128) < 64, (lane % 64) < 32
    a0, a1, a2, a3 = tiles

    def turn(x, shift):
        return pltpu.roll(x, shift, 1)

    b0 = jnp.where(low, a0, turn(a2, 64))
    b2 = jnp.where(low, turn(a0, 64), a2)
    b1 = jnp.where(low, a1, turn(a3, 64))
    b3 = jnp.where(low, turn(a1, 64), a3)
    return (
        jnp.where(even, b0, turn(b1, 32)),
        jnp.where(even, turn(b0, 96), b1),
        jnp.where(even, b2, turn(b3, 32)),
        jnp.where(even, turn(b2, 96), b3),
    )


ORDER = FIRST_AZ + LATER_AZ
EDGE = 8
CHUNK = 4


def plane_copies(flow_ref, before_refs, after_refs, ext_ref, sems):
    planes, rows, length = flow_ref.shape[1:]
    stages = []

    def put(src, place, spots, t, stage):
        dst = ext_ref.at[place, spots, t, pl.ds(EDGE, rows)]
        stages[-1].append(pltpu.make_async_copy(src, dst, sems.at[stage, place, t]))

    def layers(refs, spot, stage):
        place = 0
        for ref in refs:
            for s in range(ref.shape[0]):
                for t in range(length // LANES):
                    src = ref.at[s, :, :, pl.ds(t * LANES, LANES)]
                    put(src, place, pl.ds(spot, 2), t, stage)
                place += 1

    stages.append([])
    layers(before_refs, 0, 0)
    for c in range(planes // CHUNK):
        stages.append([])
        for place, var in enumerate(ORDER):
            for t in range(length // LANES):
                at = pl.ds(c * CHUNK, CHUNK)
                src = flow_ref.at[var, at, :, pl.ds(t * LANES, LANES)]
                put(src, place, pl.ds(c * CHUNK + 2, CHUNK), t, c + 1)
    stages.append([])
    layers(after_refs, planes + 2, planes // CHUNK + 1)
    return stages


def feed_planes(a, stages):
    @pl.when(a == 0)
    def _():
        for stage in stages:
            for c in stage:
                c.start()
        for c in stages[0] + stages[1]:
            c.wait()

    for i, stage in enumerate(stages[2:]):

        @pl.when(a == (i + 1) * CHUNK - 2)
        def _():
            for c in stage:
                c.wait()


def axial_shifts(tiles):
    lane = lax.broadcasted_iota(jnp.int32, tiles[0].shape, 1)
    count = len(tiles)
    shifts = []
    for offset in (1, -1, 2, -2):
        turned = [pltpu.roll(t, (-offset) % LANES, 1) for t in tiles]
        step = 1 if offset > 0 else -1
        outside = lane >= LANES - offset if offset > 0 else lane < -offset
        shifts.append(
            [
                jnp.where(outside, turned[t + step] if 0 <= t + step < count else 0.0, turned[t])
                for t in range(count)
            ]
        )
    return [tuple(s[t] for s in shifts) for t in range(count)]


def plane_update(part, coef, base):
    k8, k1 = SECTION_STEP * 8.0 / 12.0, SECTION_STEP / 12.0
    r1, r2 = SECTION_STEP * VISCOSITY * 16.0 / 12.0, SECTION_STEP * VISCOSITY / 12.0
    c0 = -3.0 * 30.0 / 12.0 * SECTION_STEP * VISCOSITY

    def slope(far, near, p1, m1, p2, m2):
        return near * (p1 - m1) - far * (p2 - m2)

    totals = {}
    extra = {}
    for var in (4, 2, 3, 1, 0):
        centre = part(var, 0, 0)
        axial = axial_shifts(centre)
        cycle = list(zip(*[part(var, d, 0) for d in (1, -1, 2, -2)]))
        band = list(zip(*[part(var, 0, d) for d in (1, -1, 2, -2)]))
        values = base(var)
        totals[var] = []
        for t, x in enumerate(centre):
            total = values[t] + c0 * x
            for i in range(4):
                total += coef(i) * cycle[t][i]
                total += coef(7 + i) * axial[t][i]
            total += r1 * (band[t][0] + band[t][1])
            total -= r2 * (band[t][2] + band[t][3])
            if var == 4:
                extra[1, t] = slope(coef(5), coef(4), *cycle[t])
                extra[2, t] = slope(k1, k8, *band[t])
                extra[3, t] = slope(k1, k8, *axial[t])
            elif var == 2:
                extra[0, t] = slope(k1, k8, *band[t]) + coef(6) * x
            elif var == 3:
                extra[0, t] += slope(k1, k8, *axial[t])
            elif var == 1:
                extra[0, t] += slope(coef(5), coef(4), *cycle[t])
            if var in (1, 2, 3, 0):
                total -= extra[var, t]
            totals[var].append(total)
    for t in range(len(totals[4])):
        totals[4][t] -= extra[0, t]
    return totals


def pack_kernel(flow_ref, az_first_ref, az_last_ref, rad_first_ref, rad_last_ref, edge_ref, sems, *, az, rad):
    planes, rows = flow_ref.shape[1:3]
    direct, edges = [], []
    for s, var in enumerate(rad):
        for side, start in enumerate((0, rows - 8)):
            edges.append(
                pltpu.make_async_copy(
                    flow_ref.at[var, :, pl.ds(start, 8)], edge_ref.at[side, s], sems.at[1, side, s]
                )
            )
    for s, var in enumerate(az):
        for side, (ref, start) in enumerate(((az_first_ref, 0), (az_last_ref, planes - 2))):
            direct.append(
                pltpu.make_async_copy(
                    flow_ref.at[var, pl.ds(start, 2)], ref.at[s], sems.at[0, side, s]
                )
            )
    for c in edges + direct:
        c.start()
    for c in edges:
        c.wait()
    for a in range(planes):
        for s in range(len(rad)):
            rad_first_ref[a, 2 * s : 2 * s + 2, :] = edge_ref[0, s, a, 0:2, :]
            rad_last_ref[a, 2 * s : 2 * s + 2, :] = edge_ref[1, s, a, 6:8, :]
    for c in direct:
        c.wait()


def slots_of(count_ref):
    cycle, band = lax.axis_index("azimuth"), lax.axis_index("radius")
    return cycle, band, count_ref[band, cycle]


def for_live_slots(owner_ref, count_ref, rank_ref, visit):
    cycle, band, count = slots_of(count_ref)
    for q in range(rank_ref.shape[0]):
        rank_ref[q] = 0

    def one(k, carry):
        owner = owner_ref[cycle, band, k]
        rank = rank_ref[owner]
        rank_ref[owner] = rank + 1
        visit(k, owner, rank)
        return carry

    lax.fori_loop(0, count, one, 0)


def fill_coefficients(coef_ref, mean_ref, planes):
    rows = coef_ref.shape[1]
    dt, nu = SECTION_STEP, VISCOSITY
    eye = lax.broadcasted_iota(jnp.int32, (rows, rows), 0) == lax.broadcasted_iota(
        jnp.int32, (rows, rows), 1
    )

    def column(i):
        spread = jnp.where(eye, mean_ref[i : i + 1, :], 0.0)
        return jnp.broadcast_to(jnp.sum(spread, axis=1, keepdims=True), (rows, LANES))

    cell = lax.broadcasted_iota(jnp.int32, (rows, LANES), 0) + lax.axis_index("radius") * rows
    radius_pos = cell.astype(jnp.float32) + (0.5 * rows * lax.axis_size("radius") + 0.5)
    metric = planes * lax.axis_size("azimuth") / (2.0 * math.pi) / radius_pos
    turn = column(0) * metric
    for at, speed in ((0, turn), (7, column(1))):
        coef_ref[at] = dt * (nu * 16.0 / 12.0 - speed * (8.0 / 12.0))
        coef_ref[at + 1] = dt * (nu * 16.0 / 12.0 + speed * (8.0 / 12.0))
        coef_ref[at + 2] = dt * (speed / 12.0 - nu / 12.0)
        coef_ref[at + 3] = -dt * (speed / 12.0 + nu / 12.0)
    coef_ref[4] = dt * 8.0 / 12.0 * metric
    coef_ref[5] = dt / 12.0 * metric
    coef_ref[6] = dt / radius_pos


def panels_kernel(
    owner_ref,
    count_ref,
    line_ref,
    mean_ref,
    flow_ref,
    base_ref,
    history_ref,
    out_ref,
    rows_ref,
    coef_ref,
    store_ref,
    wide_ref,
    block_ref,
    rank_ref,
    sems,
):
    planes, tiles, band = store_ref.shape[1:4]
    sources = ((flow_ref, 4), (flow_ref, 1), (flow_ref, 2), (flow_ref, 3), (base_ref, 4))
    copies = [
        pltpu.make_async_copy(
            ref.at[var, :, :, pl.ds(t * LANES, LANES)], store_ref.at[s, :, t], sems.at[s, t]
        )
        for s, (ref, var) in enumerate(sources)
        for t in range(tiles)
    ]
    for c in copies:
        c.start()
    fill_coefficients(coef_ref, mean_ref, planes)
    wide_ref[ROWS - 1] = jnp.zeros_like(wide_ref[ROWS - 1])
    for r in range(ROWS):
        width = min(LANES, history_ref.shape[1] - r * LANES)
        chunk = history_ref[:, r * LANES : r * LANES + width]
        wide_ref[r, :, 0:width] = chunk.astype(jnp.float32)
    out_ref[...] = jnp.zeros_like(out_ref)

    def place(k, owner, rank):
        for r in range(ROWS):
            block_ref[r : r + 1, :] = wide_ref[r, pl.ds(k, 1), :]
        at = pl.ds(pl.multiple_of(rank * ROWS, ROWS), ROWS)
        out_ref[owner, at, :] = block_ref[...].astype(out_ref.dtype)

    for_live_slots(owner_ref, count_ref, rank_ref, place)
    for c in copies:
        c.wait()

    lane = lax.broadcasted_iota(jnp.int32, (1, LANES), 1)
    k8, k1 = SECTION_STEP * 8.0 / 12.0, SECTION_STEP / 12.0
    r1, r2 = SECTION_STEP * VISCOSITY * 16.0 / 12.0, SECTION_STEP * VISCOSITY / 12.0

    def shifted(x, offset):
        turned = [pltpu.roll(t, (-offset) % LANES, 1) for t in x]
        zero = jnp.zeros_like(x[0])
        if offset < 0:
            return [
                jnp.where(lane < -offset, turned[t - 1] if t else zero, turned[t])
                for t in range(tiles)
            ]
        return [
            jnp.where(lane >= LANES - offset, turned[t + 1] if t + 1 < tiles else zero, turned[t])
            for t in range(tiles)
        ]

    def local(k, carry):
        line = line_ref[0, 0, k]
        la, lr = lax.div(line, band), lax.rem(line, band)

        def row(s, a, r):
            return [store_ref[s, a, t, pl.ds(r, 1), :] for t in range(tiles)]

        def coef(i, inside=None):
            value = coef_ref[i, pl.ds(lr, 1), :]
            return value if inside is None else jnp.where(inside, value, 0.0)

        center = row(0, la, lr)
        total = row(4, la, lr)

        def add(share, x):
            for t in range(tiles):
                total[t] = total[t] + share * x[t]

        add(-3.0 * 30.0 / 12.0 * SECTION_STEP * VISCOSITY, center)
        add(-coef(6), row(2, la, lr))
        turn = {1: -1.0, -1: 1.0, 2: 1.0, -2: -1.0}
        wind = row(3, la, lr)
        for i, offset in enumerate((1, -1, 2, -2)):
            far = abs(offset) == 2
            plane = la + offset
            inside = jnp.logical_and(plane >= 0, plane < planes)
            plane = jnp.clip(plane, 0, planes - 1)
            add(coef(i, inside), row(0, plane, lr))
            add(turn[offset] * coef(5 if far else 4, inside), row(1, plane, lr))
            cell = lr + offset
            inside = jnp.logical_and(cell >= 0, cell < band)
            cell = jnp.clip(cell, 0, band - 1)
            add(jnp.where(inside, -r2 if far else r1, 0.0), row(0, la, cell))
            add(jnp.where(inside, turn[offset] * (k1 if far else k8), 0.0), row(2, la, cell))
            add(coef(7 + i), shifted(center, offset))
            add(turn[offset] * (k1 if far else k8), shifted(wind, offset))
        for t in range(tiles):
            rows_ref[k, t : t + 1, :] = total[t]
        return carry

    lax.fori_loop(0, slots_of(count_ref)[2], local, 0)


def fresh_kernel(
    owner_ref,
    count_ref,
    line_ref,
    start_ref,
    coef_ref,
    rows_ref,
    before_ref,
    after_ref,
    lo_ref,
    hi_ref,
    held_ref,
    out_ref,
    ring_ref,
    sum_ref,
    rank_ref,
):
    tiles, band = ring_ref.shape[1:3]
    planes = lo_ref.shape[0]
    for s in range(2):
        for side, ref in enumerate((before_ref, after_ref)):
            for j in range(2):
                for t in range(tiles):
                    ring_ref[4 * s + 2 * side + j, t] = ref[s, j, :, t * LANES : (t + 1) * LANES]
    out_ref[...] = held_ref[...]
    lane = lax.broadcasted_iota(jnp.int32, (ROWS, LANES), 1)
    row_of = lax.broadcasted_iota(jnp.int32, (ROWS, LANES), 0)
    k8, k1 = SECTION_STEP * 8.0 / 12.0, SECTION_STEP / 12.0
    r1, r2 = SECTION_STEP * VISCOSITY * 16.0 / 12.0, SECTION_STEP * VISCOSITY / 12.0

    def shares(spot, count, near_before, far_before, near_after, far_after):
        first, second = spot == 0, spot == 1
        last, other = spot == count - 1, spot == count - 2
        return (
            jnp.where(first, far_before, 0.0),
            jnp.where(first, near_before, jnp.where(second, far_before, 0.0)),
            jnp.where(last, near_after, jnp.where(other, far_after, 0.0)),
            jnp.where(last, far_after, 0.0),
        )

    def put(k, owner, rank):
        line, start = line_ref[0, 0, k], start_ref[0, 0, k]
        la, lr = lax.div(line, band), lax.rem(line, band)
        for t in range(tiles):
            sum_ref[t : t + 1, :] = rows_ref[k, t : t + 1, :]

        @pl.when(jnp.logical_or(la < 2, la >= planes - 2))
        def _():
            c = [coef_ref[i, pl.ds(lr, 1), :] for i in range(6)]
            wind = shares(la, planes, c[4], -c[5], -c[4], c[5])
            own = shares(la, planes, c[1], c[3], c[0], c[2])
            for t in range(tiles):
                total = sum_ref[t : t + 1, :]
                for j in range(4):
                    total += wind[j] * ring_ref[j, t, pl.ds(lr, 1), :]
                    total += own[j] * ring_ref[4 + j, t, pl.ds(lr, 1), :]
                sum_ref[t : t + 1, :] = total

        @pl.when(jnp.logical_or(lr < 2, lr >= band - 2))
        def _():
            wind = shares(lr, band, k8, -k1, -k8, k1)
            own = shares(lr, band, r1, -r2, r1, -r2)
            for t in range(tiles):
                at = slice(t * LANES, (t + 1) * LANES)
                total = sum_ref[t : t + 1, :]
                for j in range(4):
                    ref = lo_ref if j < 2 else hi_ref
                    total += wind[j] * ref[la, j % 2 : j % 2 + 1, at]
                    total += own[j] * ref[la, 2 + j % 2 : 3 + j % 2, at]
                sum_ref[t : t + 1, :] = total

        tile, off = lax.div(start, LANES), lax.rem(start, LANES)
        other = jnp.minimum(tile + 1, tiles - 1)
        shift = lax.rem(2 * LANES - BP - off, LANES)
        x0 = jnp.broadcast_to(sum_ref[pl.ds(tile, 1), :], (ROWS, LANES))
        x1 = jnp.broadcast_to(sum_ref[pl.ds(other, 1), :], (ROWS, LANES))
        window = jnp.where(
            lane < 2 * LANES - BP - off, pltpu.roll(x0, shift, 1), pltpu.roll(x1, shift, 1)
        )
        at = pl.ds(pl.multiple_of(rank * ROWS, ROWS), ROWS)
        block = out_ref[owner, at, :].astype(jnp.float32)
        place = jnp.logical_and(row_of == ROWS - 1, lane >= LANES - BP)
        out_ref[owner, at, :] = jnp.where(place, window, block).astype(out_ref.dtype)

    for_live_slots(owner_ref, count_ref, rank_ref, put)


def fields_kernel(
    flow_ref,
    before0_ref,
    after0_ref,
    before1_ref,
    after1_ref,
    base_ref,
    lo0_ref,
    hi0_ref,
    lo1_ref,
    hi1_ref,
    coef_ref,
    next_ref,
    ext_ref,
    sems,
):
    a = pl.program_id(0)
    rows, length = flow_ref.shape[2:]
    tiles = length // LANES
    stages = plane_copies(
        flow_ref, (before0_ref, before1_ref), (after0_ref, after1_ref), ext_ref, sems
    )
    feed_planes(a, stages)
    for var in range(NVAR):
        if var in FIRST_RAD:
            lo, hi, s = lo0_ref, hi0_ref, FIRST_RAD.index(var)
        else:
            lo, hi, s = lo1_ref, hi1_ref, LATER_RAD.index(var)
        for t in range(tiles):
            lanes = slice(t * LANES, (t + 1) * LANES)
            place = ORDER.index(var)
            ext_ref[place, a + 2, t, EDGE - 2 : EDGE, :] = lo[a, 2 * s : 2 * s + 2, lanes]
            ext_ref[place, a + 2, t, EDGE + rows : EDGE + rows + 2, :] = hi[
                a, 2 * s : 2 * s + 2, lanes
            ]

    half = 16
    for start in range(0, rows, half):
        at = slice(start, start + half)

        def part(var, offset, row_shift):
            first = EDGE + start + row_shift
            return [
                ext_ref[ORDER.index(var), a + 2 + offset, t, first : first + half, :]
                for t in range(tiles)
            ]

        def coef(i):
            return coef_ref[i, at, :]

        def base(var):
            return [base_ref[var, 0, at, t * LANES : (t + 1) * LANES] for t in range(tiles)]

        totals = plane_update(part, coef, base)
        for var in range(NVAR):
            for t in range(tiles):
                next_ref[var, 0, at, t * LANES : (t + 1) * LANES] = totals[var][t]


ANY = pl.BlockSpec(memory_space=pltpu.HBM)
IN_SMEM = pl.BlockSpec(memory_space=pltpu.SMEM)
IN_VMEM = pl.BlockSpec(memory_space=pltpu.VMEM)
MIB = 1 << 20


def limits(mib, **more):
    return pltpu.CompilerParams(vmem_limit_bytes=mib * MIB, **more)


def cost(flops, moved):
    return pl.CostEstimate(flops=flops, bytes_accessed=moved, transcendentals=0)


def in_hbm(array):
    return pltpu.with_memory_space_constraint(array, pltpu.HBM)


def whole(array):
    shape = array.shape
    return pl.BlockSpec(shape, lambda *_: (0,) * len(shape))


def pack_call(flow, az, rad):
    _, planes, rows, length = flow.shape
    az_shape = jax.ShapeDtypeStruct((len(az), 2, rows, length), jnp.float32)
    rad_shape = jax.ShapeDtypeStruct((planes, 2 * len(rad), length), jnp.float32)
    return pl.pallas_call(
        functools.partial(pack_kernel, az=az, rad=rad),
        out_shape=(az_shape, az_shape, rad_shape, rad_shape),
        in_specs=[ANY],
        out_specs=(IN_VMEM,) * 4,
        scratch_shapes=[
            pltpu.VMEM((2, len(rad), planes, 8, length), jnp.float32),
            pltpu.SemaphoreType.DMA((2, 2, max(len(az), len(rad)))),
        ],
        compiler_params=limits(8),
        cost_estimate=cost(0, 8 * len(az) * 4 * rows * length),
    )(in_hbm(flow))


def panels_call(owner, count, line, mean_flow, flow, base, history):
    _, planes, rows, length = flow.shape
    owners, tiles = count.shape[1], length // LANES
    return pl.pallas_call(
        panels_kernel,
        name="panels",
        out_shape=(
            jax.ShapeDtypeStruct((owners, CAP * ROWS, LANES), jnp.bfloat16),
            jax.ShapeDtypeStruct((KMAX, 8, LANES), jnp.float32),
            jax.ShapeDtypeStruct((11, rows, LANES), jnp.float32),
        ),
        in_specs=[IN_SMEM] * 3 + [IN_VMEM, ANY, ANY, IN_VMEM],
        out_specs=(IN_VMEM,) * 3,
        scratch_shapes=[
            pltpu.VMEM((5, planes, tiles, rows, LANES), jnp.float32),
            pltpu.VMEM((ROWS, KMAX, LANES), jnp.float32),
            pltpu.VMEM((ROWS, LANES), jnp.float32),
            pltpu.SMEM((owners,), jnp.int32),
            pltpu.SemaphoreType.DMA((5, tiles)),
        ],
        compiler_params=limits(8),
        cost_estimate=cost(0, 5 * 4 * planes * rows * length),
    )(owner, count, line, mean_flow, in_hbm(flow), in_hbm(base), history)


def fresh_call(owner, count, line, start, coef, rows, az, rad, held):
    length = az[0].shape[-1]
    band = az[0].shape[2]
    return pl.pallas_call(
        fresh_kernel,
        name="fresh",
        out_shape=jax.ShapeDtypeStruct(held.shape, held.dtype),
        in_specs=[IN_SMEM] * 4 + [IN_VMEM] * 7,
        out_specs=IN_VMEM,
        scratch_shapes=[
            pltpu.VMEM((8, length // LANES, band, LANES), jnp.float32),
            pltpu.VMEM((8, LANES), jnp.float32),
            pltpu.SMEM((held.shape[0],), jnp.int32),
        ],
        compiler_params=limits(8),
        cost_estimate=cost(0, 4 * 4 * band * length * 4),
    )(owner, count, line, start, coef, rows, *az, *rad, held)


def fields_call(flow, az0, az1, base, rad0, rad1, coef):
    nvar, planes, rows, length = flow.shape
    cells = planes * rows * length
    every = (nvar, 1, rows, length)
    args = (in_hbm(flow), *az0, *az1, in_hbm(base), *rad0, *rad1, coef)
    return pl.pallas_call(
        fields_kernel,
        name="fields",
        out_shape=jax.ShapeDtypeStruct(flow.shape, jnp.float32),
        grid=(planes,),
        in_specs=[
            *[ANY] + [pl.BlockSpec(memory_space=pl.ANY)] * 4,
            pl.BlockSpec(every, lambda a: (0, a, 0, 0)),
            *[whole(x) for x in (*rad0, *rad1, coef)],
        ],
        out_specs=pl.BlockSpec(every, lambda a: (0, a, 0, 0)),
        scratch_shapes=[
            pltpu.VMEM(
                (nvar, planes + 4, length // LANES, rows + 2 * EDGE, LANES), jnp.float32
            ),
            pltpu.SemaphoreType.DMA((planes // CHUNK + 2, nvar, length // LANES)),
        ],
        compiler_params=limits(14, dimension_semantics=("arbitrary",)),
        cost_estimate=cost(250 * cells, 15 * 4 * cells),
    )(*args)


def weights_kernel(
    order_ref, stations_ref, weight_ref, out_ref, lhs_ref, held_ref, spot_ref, sems
):
    chunks, _, width = held_ref.shape

    def copy(i):
        at = pl.ds(pl.multiple_of(i * width, width), width)
        return pltpu.make_async_copy(weight_ref.at[:, at], held_ref.at[i], sems.at[i])

    for i in range(chunks):
        copy(i).start()

    def place(j, carry):
        spot_ref[order_ref[j]] = j
        return carry

    lax.fori_loop(0, out_ref.shape[0], place, 0, unroll=8)
    for group in range(stations_ref.shape[0] * CAP // QUADS):
        tiles = []
        for m in range(QUADS):
            source, rank = divmod(group * QUADS + m, CAP)
            tile = stations_ref[source, rank * ROWS : (rank + 1) * ROWS, :]
            tiles.append(tile.astype(jnp.float32))
        for i, tile in enumerate(swap_quads(tiles)):
            lhs_ref[i * ROWS : (i + 1) * ROWS, group * LANES : (group + 1) * LANES] = tile.astype(
                lhs_ref.dtype
            )

    groups = width // LANES

    def chunk(n, carry):
        copy(n).wait()
        part = jnp.dot(lhs_ref[...], held_ref[n], preferred_element_type=jnp.float32)
        for group in range(groups):
            lanes = slice(group * LANES, (group + 1) * LANES)
            tiles = [part[i * ROWS : (i + 1) * ROWS, lanes] for i in range(QUADS)]
            for m, tile in enumerate(swap_quads(tiles)):
                out_ref[spot_ref[(n * groups + group) * QUADS + m]] = tile
        return carry

    lax.fori_loop(0, chunks, chunk, 0)


def weights_call(order, stations, weight):
    count = order.shape[0]
    depth, observers = weight.shape
    width = 512
    return pl.pallas_call(
        weights_kernel,
        name="observers",
        out_shape=jax.ShapeDtypeStruct((count, ROWS, LANES), jnp.float32),
        in_specs=[IN_SMEM, IN_VMEM, ANY],
        out_specs=IN_VMEM,
        scratch_shapes=[
            pltpu.VMEM((NT, depth), jnp.bfloat16),
            pltpu.VMEM((observers // width, depth, width), jnp.bfloat16),
            pltpu.SMEM((count,), jnp.int32),
            pltpu.SemaphoreType.DMA((observers // width,)),
        ],
        compiler_params=limits(14),
        cost_estimate=cost(2 * NT * depth * observers, 2 * depth * observers),
    )(order, stations, in_hbm(weight))


def retard_kernel(parts_ref, matrix_ref, out_ref, times_ref, late_ref):
    def add(i, total):
        for j in range(8):
            total = total + parts_ref[i * 8 + j]
        return total

    total = lax.fori_loop(
        0, parts_ref.shape[0] // 8, add, jnp.zeros(parts_ref.shape[1:], jnp.float32)
    )
    for i in range(QUADS):
        turned = total if i == 0 else pltpu.roll(total, LANES - i * BP, 1)
        times_ref[pl.ds(i, ROWS, stride=QUADS), :] = turned
    late_ref[...] = jnp.dot(
        matrix_ref[...],
        times_ref[...],
        precision=lax.Precision.HIGHEST,
        preferred_element_type=jnp.float32,
    )
    lane = lax.broadcasted_iota(jnp.int32, (ROWS, LANES), 1)
    out = late_ref[pl.ds(0, ROWS, stride=QUADS), :]
    for i in range(1, QUADS):
        tile = pltpu.roll(late_ref[pl.ds(i, ROWS, stride=QUADS), :], i * BP, 1)
        out = jnp.where(lane >= i * BP, tile, out)
    out_ref[...] = out


def retard_call(parts, matrix):
    return pl.pallas_call(
        retard_kernel,
        name="retard",
        out_shape=jax.ShapeDtypeStruct((ROWS, LANES), jnp.float32),
        in_specs=[pl.BlockSpec(memory_space=pltpu.VMEM)] * 2,
        out_specs=pl.BlockSpec(memory_space=pltpu.VMEM),
        scratch_shapes=[pltpu.VMEM((NT, LANES), jnp.float32)] * 2,
        compiler_params=limits(4),
        cost_estimate=cost(2 * parts.size, 4 * parts.size),
    )(parts, matrix)


def exchange(first, last, axis, wrap):
    count = lax.axis_size(axis)
    up = [(i, (i + 1) % count) for i in range(count if wrap else count - 1)]
    down = [(j, i) for i, j in up]
    return lax.ppermute(last, axis, up), lax.ppermute(first, axis, down)


def neighbours(packed):
    az_first, az_last, rad_first, rad_last = packed
    rad = exchange(rad_first, rad_last, "radius", False)
    az = exchange(az_first, az_last, "azimuth", True)
    return az, rad


def per_device(
    flow_state,
    base_state,
    mean_flow,
    panel_history,
    panel_line,
    panel_start,
    panel_count,
    panel_owner,
    source_weight,
    retarded_time,
    observer_block,
):
    az0, rad0 = neighbours(pack_call(flow_state, FIRST_AZ, FIRST_RAD))
    slots = (panel_owner, panel_count.T)
    history, local, coef = panels_call(
        *slots, panel_line, mean_flow, flow_state, base_state, panel_history[0, 0]
    )
    outgoing = fresh_call(*slots, panel_line, panel_start, coef, local, az0, rad0, history)
    stations = lax.all_to_all(outgoing, "azimuth", split_axis=0, concat_axis=0, tiled=True)
    later, _ = lax.optimization_barrier((flow_state, outgoing))
    packed = pack_call(later, LATER_AZ, LATER_RAD)
    az1, rad1 = neighbours(packed)
    sends = weights_call(observer_block, stations, source_weight[0])
    parts = lax.all_to_all(sends, BOTH, split_axis=0, concat_axis=0, tiled=True)
    next_state = fields_call(flow_state, az0, az1, base_state, rad0, rad1, coef)

    chosen = lax.dynamic_index_in_dim(observer_block, lax.axis_index(BOTH), 0, keepdims=False)
    blocks = lax.broadcasted_iota(jnp.int32, retarded_time.shape, 0)
    matrix = jnp.sum(jnp.where(blocks == chosen, retarded_time, 0.0), axis=0)
    pressure = retard_call(parts, matrix)
    return next_state, pressure.reshape(1, ROWS * LANES)


def solution(mesh):
    placed = (
        P(None, "azimuth", "radius", None),
        P(None, "azimuth", "radius", None),
        P(None, "radius"),
        P("azimuth", "radius", None, None),
        P("azimuth", "radius", None),
        P("azimuth", "radius", None),
        P(),
        P(),
        P("radius", "azimuth", None),
        P(),
        P(),
    )

    return jax.shard_map(
        per_device,
        mesh=mesh,
        in_specs=placed,
        out_specs=(P(None, "azimuth", "radius", None), P(BOTH, None)),
        check_vma=False,
    )
```

```python
import functools
import math

import jax
import jax.numpy as jnp
from jax import lax
from jax.experimental import pallas as pl
from jax.experimental.pallas import tpu as pltpu
from jax.sharding import PartitionSpec as P

NT = 64
BP = 32
KMAX = 16
CAP = 2
LANES = 128
ROWS = NT * BP // LANES
QUADS = LANES // BP
WIDTH = 512

SECTION_STEP = 0.3
VISCOSITY = 0.05
BOTH = ("azimuth", "radius")

NVAR = 5
FIRST_RAD = (2, 4)
LATER_RAD = (0, 1, 3)


def swap_quads(tiles):
    lane = lax.broadcasted_iota(jnp.int32, tiles[0].shape, 1)
    low, even = (lane % 128) < 64, (lane % 64) < 32
    a0, a1, a2, a3 = tiles

    def turn(x, shift):
        return pltpu.roll(x, shift, 1)

    b0 = jnp.where(low, a0, turn(a2, 64))
    b2 = jnp.where(low, turn(a0, 64), a2)
    b1 = jnp.where(low, a1, turn(a3, 64))
    b3 = jnp.where(low, turn(a1, 64), a3)
    return (
        jnp.where(even, b0, turn(b1, 32)),
        jnp.where(even, turn(b0, 96), b1),
        jnp.where(even, b2, turn(b3, 32)),
        jnp.where(even, turn(b2, 96), b3),
    )


EDGE = 8
CHUNK = 4


def plane_copies(flow_ref, before_ref, after_ref, ext_ref, sems):
    planes, rows, length = flow_ref.shape[1:]
    sources = [(before_ref, 0, 0, 2)]
    for first in range(0, planes, CHUNK):
        sources.append((flow_ref, first, first + 2, CHUNK))
    sources.append((after_ref, 0, planes + 2, 2))
    stages = []
    for stage, (ref, first, spot, count) in enumerate(sources):
        stages.append([])
        for var in range(NVAR):
            for t in range(length // LANES):
                src = ref.at[var, pl.ds(first, count), :, pl.ds(t * LANES, LANES)]
                dst = ext_ref.at[var, pl.ds(spot, count), t, pl.ds(EDGE, rows)]
                stages[-1].append(pltpu.make_async_copy(src, dst, sems.at[stage, var, t]))
    return stages


def axial_shifts(tiles):
    lane = lax.broadcasted_iota(jnp.int32, tiles[0].shape, 1)
    count = len(tiles)
    shifts = []
    for offset in (1, -1, 2, -2):
        turned = [pltpu.roll(t, (-offset) % LANES, 1) for t in tiles]
        step = 1 if offset > 0 else -1
        outside = lane >= LANES - offset if offset > 0 else lane < -offset
        shifts.append(
            [
                jnp.where(outside, turned[t + step] if 0 <= t + step < count else 0.0, turned[t])
                for t in range(count)
            ]
        )
    return [tuple(s[t] for s in shifts) for t in range(count)]


def plane_update(part, coef, base):
    k8, k1 = SECTION_STEP * 8.0 / 12.0, SECTION_STEP / 12.0
    r1, r2 = SECTION_STEP * VISCOSITY * 16.0 / 12.0, SECTION_STEP * VISCOSITY / 12.0
    c0 = -3.0 * 30.0 / 12.0 * SECTION_STEP * VISCOSITY

    def slope(far, near, p1, m1, p2, m2):
        return near * (p1 - m1) - far * (p2 - m2)

    totals = {}
    extra = {}
    for var in (4, 2, 3, 1, 0):
        centre = part(var, 0, 0)
        axial = axial_shifts(centre)
        cycle = list(zip(*[part(var, d, 0) for d in (1, -1, 2, -2)]))
        band = list(zip(*[part(var, 0, d) for d in (1, -1, 2, -2)]))
        values = base(var)
        totals[var] = []
        for t, x in enumerate(centre):
            total = values[t] + c0 * x
            for i in range(4):
                total += coef(i) * cycle[t][i]
                total += coef(7 + i) * axial[t][i]
            total += r1 * (band[t][0] + band[t][1])
            total -= r2 * (band[t][2] + band[t][3])
            if var == 4:
                extra[1, t] = slope(coef(5), coef(4), *cycle[t])
                extra[2, t] = slope(k1, k8, *band[t])
                extra[3, t] = slope(k1, k8, *axial[t])
            elif var == 2:
                extra[0, t] = slope(k1, k8, *band[t]) + coef(6) * x
            elif var == 3:
                extra[0, t] += slope(k1, k8, *axial[t])
            elif var == 1:
                extra[0, t] += slope(coef(5), coef(4), *cycle[t])
            if var in (1, 2, 3, 0):
                total -= extra[var, t]
            totals[var].append(total)
    for t in range(len(totals[4])):
        totals[4][t] -= extra[0, t]
    return totals


def pack_kernel(flow_ref, *refs, rad, with_az):
    *outs, edge_ref, sems = refs
    rad_first_ref, rad_last_ref = outs[-2:]
    planes, rows = flow_ref.shape[1:3]
    direct, edges = [], []
    for s, var in enumerate(rad):
        for side, start in enumerate((0, rows - EDGE)):
            edges.append(
                pltpu.make_async_copy(
                    flow_ref.at[var, :, pl.ds(start, EDGE)],
                    edge_ref.at[side, s],
                    sems.at[side, s],
                )
            )
    if with_az:
        for side, (ref, start) in enumerate(zip(outs, (0, planes - 2))):
            direct.append(
                pltpu.make_async_copy(
                    flow_ref.at[:, pl.ds(start, 2)], ref, sems.at[side, len(rad)]
                )
            )
    for c in edges + direct:
        c.start()
    for c in edges:
        c.wait()
    for a in range(planes):
        for s in range(len(rad)):
            rad_first_ref[a, 2 * s : 2 * s + 2, :] = edge_ref[0, s, a, 0:2, :]
            rad_last_ref[a, 2 * s : 2 * s + 2, :] = edge_ref[1, s, a, EDGE - 2 : EDGE, :]
    for c in direct:
        c.wait()


def fill_coefficients(coef_ref, mean_ref, planes):
    rows = coef_ref.shape[1]
    dt, nu = SECTION_STEP, VISCOSITY
    eye = lax.broadcasted_iota(jnp.int32, (rows, rows), 0) == lax.broadcasted_iota(
        jnp.int32, (rows, rows), 1
    )

    def column(i):
        spread = jnp.where(eye, mean_ref[i : i + 1, :], 0.0)
        return jnp.broadcast_to(jnp.sum(spread, axis=1, keepdims=True), (rows, LANES))

    cell = lax.broadcasted_iota(jnp.int32, (rows, LANES), 0) + lax.axis_index("radius") * rows
    radius_pos = cell.astype(jnp.float32) + (0.5 * rows * lax.axis_size("radius") + 0.5)
    metric = planes * lax.axis_size("azimuth") / (2.0 * math.pi) / radius_pos
    turn = column(0) * metric
    for at, speed in ((0, turn), (7, column(1))):
        coef_ref[at] = dt * (nu * 16.0 / 12.0 - speed * (8.0 / 12.0))
        coef_ref[at + 1] = dt * (nu * 16.0 / 12.0 + speed * (8.0 / 12.0))
        coef_ref[at + 2] = dt * (speed / 12.0 - nu / 12.0)
        coef_ref[at + 3] = -dt * (speed / 12.0 + nu / 12.0)
    coef_ref[4] = dt * 8.0 / 12.0 * metric
    coef_ref[5] = dt / 12.0 * metric
    coef_ref[6] = dt / radius_pos


def panels_kernel(
    owner_ref,
    count_ref,
    line_ref,
    mean_ref,
    flow_ref,
    base_ref,
    history_ref,
    out_ref,
    rows_ref,
    coef_ref,
    slots_ref,
    store_ref,
    wide_ref,
    block_ref,
    rank_ref,
    own_ref,
    sems,
):
    planes, tiles, band = store_ref.shape[1:4]
    sources = ((flow_ref, 4), (flow_ref, 1), (flow_ref, 2), (flow_ref, 3), (base_ref, 4))
    copies = [
        pltpu.make_async_copy(
            ref.at[var, :, :, pl.ds(t * LANES, LANES)], store_ref.at[s, :, t], sems.at[s, t]
        )
        for s, (ref, var) in enumerate(sources)
        for t in range(tiles)
    ]
    cycle, radius = lax.axis_index("azimuth"), lax.axis_index("radius")
    owners = pltpu.make_async_copy(owner_ref.at[cycle], own_ref, sems.at[len(sources), 0])
    owners.start()
    for c in copies:
        c.start()
    count = count_ref[radius, cycle]
    slots_ref[2 * KMAX] = count
    fill_coefficients(coef_ref, mean_ref, planes)
    wide_ref[ROWS - 1] = jnp.zeros_like(wide_ref[ROWS - 1])
    for r in range(ROWS):
        width = min(LANES, history_ref.shape[1] - r * LANES)
        chunk = history_ref[:, r * LANES : r * LANES + width]
        wide_ref[r, :, 0:width] = chunk.astype(jnp.float32)
    out_ref[...] = jnp.zeros_like(out_ref)

    for q in range(rank_ref.shape[0]):
        rank_ref[q] = 0
    owners.wait()

    def place(k, carry):
        owner = own_ref[radius, k]
        rank = rank_ref[owner]
        rank_ref[owner] = rank + 1
        slots_ref[k] = owner
        slots_ref[KMAX + k] = rank
        for r in range(ROWS):
            block_ref[r : r + 1, :] = wide_ref[r, pl.ds(k, 1), :]
        at = pl.ds(pl.multiple_of(rank * ROWS, ROWS), ROWS)
        out_ref[owner, at, :] = block_ref[...].astype(out_ref.dtype)
        return carry

    lax.fori_loop(0, count, place, 0)
    for c in copies:
        c.wait()

    lane = lax.broadcasted_iota(jnp.int32, (1, LANES), 1)
    k8, k1 = SECTION_STEP * 8.0 / 12.0, SECTION_STEP / 12.0
    r1, r2 = SECTION_STEP * VISCOSITY * 16.0 / 12.0, SECTION_STEP * VISCOSITY / 12.0

    def shifted(x, offset):
        turned = [pltpu.roll(t, (-offset) % LANES, 1) for t in x]
        zero = jnp.zeros_like(x[0])
        if offset < 0:
            return [
                jnp.where(lane < -offset, turned[t - 1] if t else zero, turned[t])
                for t in range(tiles)
            ]
        return [
            jnp.where(lane >= LANES - offset, turned[t + 1] if t + 1 < tiles else zero, turned[t])
            for t in range(tiles)
        ]

    def local(k, carry):
        line = line_ref[0, 0, k]
        la, lr = lax.div(line, band), lax.rem(line, band)

        def row(s, a, r):
            return [store_ref[s, a, t, pl.ds(r, 1), :] for t in range(tiles)]

        def coef(i, inside=None):
            value = coef_ref[i, pl.ds(lr, 1), :]
            return value if inside is None else jnp.where(inside, value, 0.0)

        center = row(0, la, lr)
        total = row(4, la, lr)

        def add(share, x):
            for t in range(tiles):
                total[t] = total[t] + share * x[t]

        add(-3.0 * 30.0 / 12.0 * SECTION_STEP * VISCOSITY, center)
        add(-coef(6), row(2, la, lr))
        turn = {1: -1.0, -1: 1.0, 2: 1.0, -2: -1.0}
        wind = row(3, la, lr)
        for i, offset in enumerate((1, -1, 2, -2)):
            far = abs(offset) == 2
            plane = la + offset
            inside = jnp.logical_and(plane >= 0, plane < planes)
            plane = jnp.clip(plane, 0, planes - 1)
            add(coef(i, inside), row(0, plane, lr))
            add(turn[offset] * coef(5 if far else 4, inside), row(1, plane, lr))
            cell = lr + offset
            inside = jnp.logical_and(cell >= 0, cell < band)
            cell = jnp.clip(cell, 0, band - 1)
            add(jnp.where(inside, -r2 if far else r1, 0.0), row(0, la, cell))
            add(jnp.where(inside, turn[offset] * (k1 if far else k8), 0.0), row(2, la, cell))
            add(coef(7 + i), shifted(center, offset))
            add(turn[offset] * (k1 if far else k8), shifted(wind, offset))
        for t in range(tiles):
            rows_ref[k, t : t + 1, :] = total[t]
        return carry

    lax.fori_loop(0, count, local, 0)


def fresh_kernel(
    slots_ref,
    line_ref,
    start_ref,
    coef_ref,
    rows_ref,
    before_ref,
    after_ref,
    lo_ref,
    hi_ref,
    held_ref,
    out_ref,
    ring_ref,
    sum_ref,
    sems,
):
    tiles, band = ring_ref.shape[1:3]
    planes = lo_ref.shape[0]
    copies = []
    for s, var in enumerate((1, 4)):
        for side, ref in enumerate((before_ref, after_ref)):
            for t in range(tiles):
                src = ref.at[var, :, :, pl.ds(t * LANES, LANES)]
                dst = ring_ref.at[pl.ds(4 * s + 2 * side, 2), t]
                copies.append(pltpu.make_async_copy(src, dst, sems.at[s, side, t]))
    for c in copies:
        c.start()
    out_ref[...] = held_ref[...]
    lane = lax.broadcasted_iota(jnp.int32, (ROWS, LANES), 1)
    row_of = lax.broadcasted_iota(jnp.int32, (ROWS, LANES), 0)
    k8, k1 = SECTION_STEP * 8.0 / 12.0, SECTION_STEP / 12.0
    r1, r2 = SECTION_STEP * VISCOSITY * 16.0 / 12.0, SECTION_STEP * VISCOSITY / 12.0

    def shares(spot, count, near_before, far_before, near_after, far_after):
        first, second = spot == 0, spot == 1
        last, other = spot == count - 1, spot == count - 2
        return (
            jnp.where(first, far_before, 0.0),
            jnp.where(first, near_before, jnp.where(second, far_before, 0.0)),
            jnp.where(last, near_after, jnp.where(other, far_after, 0.0)),
            jnp.where(last, far_after, 0.0),
        )

    def put(k, carry):
        owner, rank = slots_ref[k], slots_ref[KMAX + k]
        line, start = line_ref[0, 0, k], start_ref[0, 0, k]
        la, lr = lax.div(line, band), lax.rem(line, band)
        for t in range(tiles):
            sum_ref[t : t + 1, :] = rows_ref[k, t : t + 1, :]

        @pl.when(jnp.logical_or(la < 2, la >= planes - 2))
        def _():
            c = [coef_ref[i, pl.ds(lr, 1), :] for i in range(6)]
            wind = shares(la, planes, c[4], -c[5], -c[4], c[5])
            own = shares(la, planes, c[1], c[3], c[0], c[2])
            for t in range(tiles):
                total = sum_ref[t : t + 1, :]
                for j in range(4):
                    total += wind[j] * ring_ref[j, t, pl.ds(lr, 1), :]
                    total += own[j] * ring_ref[4 + j, t, pl.ds(lr, 1), :]
                sum_ref[t : t + 1, :] = total

        @pl.when(jnp.logical_or(lr < 2, lr >= band - 2))
        def _():
            wind = shares(lr, band, k8, -k1, -k8, k1)
            own = shares(lr, band, r1, -r2, r1, -r2)
            for t in range(tiles):
                at = slice(t * LANES, (t + 1) * LANES)
                total = sum_ref[t : t + 1, :]
                for j in range(4):
                    ref = lo_ref if j < 2 else hi_ref
                    total += wind[j] * ref[la, j % 2 : j % 2 + 1, at]
                    total += own[j] * ref[la, 2 + j % 2 : 3 + j % 2, at]
                sum_ref[t : t + 1, :] = total

        tile, off = lax.div(start, LANES), lax.rem(start, LANES)
        other = jnp.minimum(tile + 1, tiles - 1)
        shift = lax.rem(2 * LANES - BP - off, LANES)
        x0 = jnp.broadcast_to(sum_ref[pl.ds(tile, 1), :], (ROWS, LANES))
        x1 = jnp.broadcast_to(sum_ref[pl.ds(other, 1), :], (ROWS, LANES))
        window = jnp.where(
            lane < 2 * LANES - BP - off, pltpu.roll(x0, shift, 1), pltpu.roll(x1, shift, 1)
        )
        at = pl.ds(pl.multiple_of(rank * ROWS, ROWS), ROWS)
        block = out_ref[owner, at, :].astype(jnp.float32)
        place = jnp.logical_and(row_of == ROWS - 1, lane >= LANES - BP)
        out_ref[owner, at, :] = jnp.where(place, window, block).astype(out_ref.dtype)
        return carry

    for c in copies:
        c.wait()
    lax.fori_loop(0, slots_ref[2 * KMAX], put, 0)


def fields_kernel(
    flow_ref,
    before_ref,
    after_ref,
    base_ref,
    lo0_ref,
    hi0_ref,
    lo1_ref,
    hi1_ref,
    coef_ref,
    next_ref,
    ext_ref,
    sems,
):
    group = pl.program_id(0)
    planes, rows, length = flow_ref.shape[1:]
    tiles = length // LANES
    stages = plane_copies(flow_ref, before_ref, after_ref, ext_ref, sems)

    def radial_layers(plane, carry):
        for var in range(NVAR):
            if var in FIRST_RAD:
                lo, hi, s = lo0_ref, hi0_ref, FIRST_RAD.index(var)
            else:
                lo, hi, s = lo1_ref, hi1_ref, LATER_RAD.index(var)
            for t in range(tiles):
                at = slice(2 * s, 2 * s + 2), slice(t * LANES, (t + 1) * LANES)
                ext_ref[var, plane + 2, t, EDGE - 2 : EDGE, :] = lo[(plane, *at)]
                ext_ref[var, plane + 2, t, EDGE + rows : EDGE + rows + 2, :] = hi[(plane, *at)]
        return carry

    @pl.when(group == 0)
    def _():
        for stage in stages:
            for c in stage:
                c.start()
        lax.fori_loop(0, planes, radial_layers, 0)
        for c in stages[0] + stages[1]:
            c.wait()

    def one(inner, carry):
        a = group * CHUNK + inner
        for i, stage in enumerate(stages[2:]):

            @pl.when(a == (i + 1) * CHUNK - 2)
            def _():
                for c in stage:
                    c.wait()

        half = 8
        for start in range(0, rows, half):
            at = slice(start, start + half)

            def part(var, offset, row_shift):
                first = EDGE + start + row_shift
                return [
                    ext_ref[var, a + 2 + offset, t, first : first + half, :] for t in range(tiles)
                ]

            held = [coef_ref[i, at, :] for i in range(coef_ref.shape[0])]

            def base(var):
                return [
                    base_ref[var, inner, at, t * LANES : (t + 1) * LANES] for t in range(tiles)
                ]

            totals = plane_update(part, held.__getitem__, base)
            for var in range(NVAR):
                for t in range(tiles):
                    next_ref[var, inner, at, t * LANES : (t + 1) * LANES] = totals[var][t]
        return carry

    lax.fori_loop(0, CHUNK, one, 0)


ANY = pl.BlockSpec(memory_space=pltpu.HBM)
IN_SMEM = pl.BlockSpec(memory_space=pltpu.SMEM)
IN_VMEM = pl.BlockSpec(memory_space=pltpu.VMEM)
MIB = 1 << 20


def limits(mib, **more):
    return pltpu.CompilerParams(vmem_limit_bytes=mib * MIB, **more)


def cost(flops, moved):
    return pl.CostEstimate(flops=flops, bytes_accessed=moved, transcendentals=0)


def in_hbm(array):
    return pltpu.with_memory_space_constraint(array, pltpu.HBM)


def whole(array):
    shape = array.shape
    return pl.BlockSpec(shape, lambda *_: (0,) * len(shape))


def pack_call(flow, rad, with_az):
    nvar, planes, rows, length = flow.shape
    az_shape = jax.ShapeDtypeStruct((nvar, 2, rows, length), jnp.float32)
    rad_shape = jax.ShapeDtypeStruct((planes, 2 * len(rad), length), jnp.float32)
    shapes = (az_shape,) * (2 * with_az) + (rad_shape,) * 2
    return pl.pallas_call(
        functools.partial(pack_kernel, rad=rad, with_az=with_az),
        out_shape=shapes,
        in_specs=[ANY],
        out_specs=(IN_VMEM,) * len(shapes),
        scratch_shapes=[
            pltpu.VMEM((2, len(rad), planes, EDGE, length), jnp.float32),
            pltpu.SemaphoreType.DMA((2, len(rad) + 1)),
        ],
        compiler_params=limits(8),
        cost_estimate=cost(0, 20 * MIB),
    )(in_hbm(flow))


def panels_call(owner, count, line, mean_flow, flow, base, history):
    _, planes, rows, length = flow.shape
    owners, tiles = count.shape[1], length // LANES
    return pl.pallas_call(
        panels_kernel,
        name="panels",
        out_shape=(
            jax.ShapeDtypeStruct((owners, CAP * ROWS, LANES), jnp.bfloat16),
            jax.ShapeDtypeStruct((KMAX, 8, LANES), jnp.float32),
            jax.ShapeDtypeStruct((11, rows, LANES), jnp.float32),
            jax.ShapeDtypeStruct((LANES,), jnp.int32),
        ),
        in_specs=[ANY, IN_SMEM, IN_SMEM, IN_VMEM, ANY, ANY, IN_VMEM],
        out_specs=(IN_VMEM,) * 3 + (IN_SMEM,),
        scratch_shapes=[
            pltpu.VMEM((5, planes, tiles, rows, LANES), jnp.float32),
            pltpu.VMEM((ROWS, KMAX, LANES), jnp.float32),
            pltpu.VMEM((ROWS, LANES), jnp.float32),
            pltpu.SMEM((owners,), jnp.int32),
            pltpu.SMEM(owner.shape[1:], jnp.int32),
            pltpu.SemaphoreType.DMA((6, tiles)),
        ],
        compiler_params=limits(8),
        cost_estimate=cost(0, 5 * 4 * planes * rows * length),
    )(in_hbm(owner), count, line, mean_flow, in_hbm(flow), in_hbm(base), history)


def fresh_call(slots, line, start, coef, rows, az, rad, held):
    length = az[0].shape[-1]
    band = az[0].shape[2]
    return pl.pallas_call(
        fresh_kernel,
        name="fresh",
        out_shape=jax.ShapeDtypeStruct(held.shape, held.dtype),
        in_specs=[IN_SMEM] * 3 + [IN_VMEM] * 2 + [pl.BlockSpec(memory_space=pl.ANY)] * 2 + [IN_VMEM] * 3,
        out_specs=IN_VMEM,
        scratch_shapes=[
            pltpu.VMEM((8, length // LANES, band, LANES), jnp.float32),
            pltpu.VMEM((8, LANES), jnp.float32),
            pltpu.SemaphoreType.DMA((2, 2, length // LANES)),
        ],
        compiler_params=limits(8),
        cost_estimate=cost(0, 4 * 4 * band * length * 4),
    )(slots, line, start, coef, rows, *az, *rad, held)


def fields_call(flow, az, base, rad0, rad1, coef):
    nvar, planes, rows, length = flow.shape
    cells = planes * rows * length
    every = (nvar, CHUNK, rows, length)
    args = (in_hbm(flow), *az, in_hbm(base), *rad0, *rad1, coef)
    return pl.pallas_call(
        fields_kernel,
        name="fields",
        out_shape=jax.ShapeDtypeStruct(flow.shape, jnp.float32),
        grid=(planes // CHUNK,),
        in_specs=[
            *[ANY] + [pl.BlockSpec(memory_space=pl.ANY)] * 2,
            pl.BlockSpec(every, lambda a: (0, a, 0, 0)),
            *[whole(x) for x in (*rad0, *rad1, coef)],
        ],
        out_specs=pl.BlockSpec(every, lambda a: (0, a, 0, 0)),
        scratch_shapes=[
            pltpu.VMEM(
                (nvar, planes + 4, length // LANES, rows + 2 * EDGE, LANES), jnp.float32
            ),
            pltpu.SemaphoreType.DMA((planes // CHUNK + 2, nvar, length // LANES)),
        ],
        compiler_params=limits(18, dimension_semantics=("arbitrary",)),
        cost_estimate=cost(250 * cells, 15 * 4 * cells),
    )(*args)


def weights_kernel(
    order_ref, stations_ref, weight_ref, out_ref, mask_ref, lhs_ref, held_ref, spot_ref, sems
):
    chunks, _, width = held_ref.shape
    copies = [
        pltpu.make_async_copy(
            weight_ref.at[:, pl.ds(i * width, width)], held_ref.at[i], sems.at[i]
        )
        for i in range(chunks)
    ]
    for c in copies:
        c.start()
    mine = order_ref[lax.axis_index("azimuth") * lax.axis_size("radius") + lax.axis_index("radius")]
    block = lax.broadcasted_iota(jnp.int32, mask_ref.shape, 1)
    mask_ref[...] = jnp.where(block == mine, 1.0, 0.0)

    def place(j, carry):
        spot_ref[order_ref[j]] = j
        return carry

    lax.fori_loop(0, out_ref.shape[0], place, 0, unroll=8)
    for group in range(stations_ref.shape[0] * CAP // QUADS):
        tiles = []
        for m in range(QUADS):
            source, rank = divmod(group * QUADS + m, CAP)
            tile = stations_ref[source, rank * ROWS : (rank + 1) * ROWS, :]
            tiles.append(tile.astype(jnp.float32))
        for i, tile in enumerate(swap_quads(tiles)):
            lhs_ref[i * ROWS : (i + 1) * ROWS, group * LANES : (group + 1) * LANES] = tile.astype(
                lhs_ref.dtype
            )

    groups = width // LANES
    for n, c in enumerate(copies):
        c.wait()
        part = jnp.dot(lhs_ref[...], held_ref[n], preferred_element_type=jnp.float32)
        for group in range(groups):
            lanes = slice(group * LANES, (group + 1) * LANES)
            tiles = [part[i * ROWS : (i + 1) * ROWS, lanes] for i in range(QUADS)]
            for m, tile in enumerate(swap_quads(tiles)):
                out_ref[spot_ref[(n * groups + group) * QUADS + m]] = tile


def weights_call(order, stations, weight):
    count = order.shape[0]
    depth, observers = weight.shape
    return pl.pallas_call(
        weights_kernel,
        name="observers",
        out_shape=(
            jax.ShapeDtypeStruct((count, ROWS, LANES), jnp.float32),
            jax.ShapeDtypeStruct((1, count), jnp.float32),
        ),
        in_specs=[IN_SMEM, IN_VMEM, ANY],
        out_specs=(IN_VMEM, IN_VMEM),
        scratch_shapes=[
            pltpu.VMEM((NT, depth), jnp.bfloat16),
            pltpu.VMEM((observers // WIDTH, depth, WIDTH), jnp.bfloat16),
            pltpu.SMEM((count,), jnp.int32),
            pltpu.SemaphoreType.DMA((observers // WIDTH,)),
        ],
        compiler_params=limits(14),
        cost_estimate=cost(2 * NT * depth * observers, 2 * depth * observers),
    )(order, stations, in_hbm(weight))


def retard_kernel(parts_ref, matrix_ref, out_ref, times_ref, late_ref):
    def add(i, total):
        for j in range(8):
            total = total + parts_ref[i * 8 + j]
        return total

    total = lax.fori_loop(
        0, parts_ref.shape[0] // 8, add, jnp.zeros(parts_ref.shape[1:], jnp.float32)
    )
    for i in range(QUADS):
        turned = total if i == 0 else pltpu.roll(total, LANES - i * BP, 1)
        times_ref[pl.ds(i, ROWS, stride=QUADS), :] = turned
    late_ref[...] = jnp.dot(
        matrix_ref[...],
        times_ref[...],
        precision=lax.Precision.HIGHEST,
        preferred_element_type=jnp.float32,
    )
    lane = lax.broadcasted_iota(jnp.int32, (ROWS, LANES), 1)
    out = late_ref[pl.ds(0, ROWS, stride=QUADS), :]
    for i in range(1, QUADS):
        tile = pltpu.roll(late_ref[pl.ds(i, ROWS, stride=QUADS), :], i * BP, 1)
        out = jnp.where(lane >= i * BP, tile, out)
    out_ref[...] = out


def retard_call(parts, matrix):
    return pl.pallas_call(
        retard_kernel,
        name="retard",
        out_shape=jax.ShapeDtypeStruct((ROWS, LANES), jnp.float32),
        in_specs=[pl.BlockSpec(memory_space=pltpu.VMEM)] * 2,
        out_specs=pl.BlockSpec(memory_space=pltpu.VMEM),
        scratch_shapes=[pltpu.VMEM((NT, LANES), jnp.float32)] * 2,
        compiler_params=limits(4),
        cost_estimate=cost(2 * parts.size, 4 * parts.size),
    )(parts, matrix)


def exchange(first, last, axis, wrap):
    count = lax.axis_size(axis)
    up = [(i, (i + 1) % count) for i in range(count if wrap else count - 1)]
    down = [(j, i) for i, j in up]
    return lax.ppermute(last, axis, up), lax.ppermute(first, axis, down)


def per_device(
    flow_state,
    base_state,
    mean_flow,
    panel_history,
    panel_line,
    panel_start,
    panel_count,
    panel_owner,
    source_weight,
    retarded_time,
    observer_block,
):
    az_first, az_last, *ends = pack_call(flow_state, FIRST_RAD, True)
    az = exchange(az_first, az_last, "azimuth", True)
    rad0 = exchange(*ends, "radius", False)
    history, local, coef, slots = panels_call(
        panel_owner,
        panel_count.T,
        panel_line,
        mean_flow,
        flow_state,
        base_state,
        panel_history[0, 0],
    )
    outgoing = fresh_call(slots, panel_line, panel_start, coef, local, az, rad0, history)
    stations = lax.all_to_all(outgoing, "azimuth", split_axis=0, concat_axis=0, tiled=True)
    later, _ = lax.optimization_barrier((flow_state, outgoing))
    packed = pack_call(later, LATER_RAD, False)
    rad1 = exchange(*packed, "radius", False)
    sends, mask = weights_call(observer_block, stations, source_weight[0])
    parts = lax.all_to_all(sends, BOTH, split_axis=0, concat_axis=0, tiled=True)
    next_state = fields_call(flow_state, az, base_state, rad0, rad1, coef)

    matrix = jnp.sum(retarded_time * mask[0][:, None, None], axis=0)
    pressure = retard_call(parts, matrix)
    return next_state, pressure.reshape(1, ROWS * LANES)


def solution(mesh):
    placed = (
        P(None, "azimuth", "radius", None),
        P(None, "azimuth", "radius", None),
        P(None, "radius"),
        P("azimuth", "radius", None, None),
        P("azimuth", "radius", None),
        P("azimuth", "radius", None),
        P(),
        P(),
        P("radius", "azimuth", None),
        P(),
        P(),
    )

    return jax.shard_map(
        per_device,
        mesh=mesh,
        in_specs=placed,
        out_specs=(P(None, "azimuth", "radius", None), P(BOTH, None)),
        check_vma=False,
    )
```

```python
import functools
import math

import jax
import jax.numpy as jnp
from jax import lax
from jax.experimental import pallas as pl
from jax.experimental.pallas import tpu as pltpu
from jax.sharding import PartitionSpec as P

NT = 64
BP = 32
KMAX = 16
CAP = 2
LANES = 128
ROWS = NT * BP // LANES
QUADS = LANES // BP
WIRE_SCALE = 64.0
WIDTH = 1024

SECTION_STEP = 0.3
VISCOSITY = 0.05
BOTH = ("azimuth", "radius")

NVAR = 5
FIRST_RAD = (2, 4)
LATER_RAD = (0, 1, 3)


def swap_quads(tiles):
    lane = lax.broadcasted_iota(jnp.int32, tiles[0].shape, 1)
    low, even = (lane % 128) < 64, (lane % 64) < 32
    a0, a1, a2, a3 = tiles

    def turn(x, shift):
        return pltpu.roll(x, shift, 1)

    b0 = jnp.where(low, a0, turn(a2, 64))
    b2 = jnp.where(low, turn(a0, 64), a2)
    b1 = jnp.where(low, a1, turn(a3, 64))
    b3 = jnp.where(low, turn(a1, 64), a3)
    return (
        jnp.where(even, b0, turn(b1, 32)),
        jnp.where(even, turn(b0, 96), b1),
        jnp.where(even, b2, turn(b3, 32)),
        jnp.where(even, turn(b2, 96), b3),
    )


EDGE = 8
CHUNK = 4


def plane_copies(flow_ref, before_ref, after_ref, ext_ref, sems):
    planes, rows, length = flow_ref.shape[1:]
    sources = [(before_ref, 0, 0, 2)]
    for first in range(0, planes, CHUNK):
        sources.append((flow_ref, first, first + 2, CHUNK))
    sources.append((after_ref, 0, planes + 2, 2))
    stages = []
    for stage, (ref, first, spot, count) in enumerate(sources):
        stages.append([])
        for var in range(NVAR):
            for t in range(length // LANES):
                src = ref.at[var, pl.ds(first, count), :, pl.ds(t * LANES, LANES)]
                dst = ext_ref.at[var, pl.ds(spot, count), t, pl.ds(EDGE, rows)]
                stages[-1].append(pltpu.make_async_copy(src, dst, sems.at[stage, var, t]))
    return stages


def axial_shifts(tiles):
    lane = lax.broadcasted_iota(jnp.int32, tiles[0].shape, 1)
    count = len(tiles)
    shifts = []
    for offset in (1, -1, 2, -2):
        turned = [pltpu.roll(t, (-offset) % LANES, 1) for t in tiles]
        step = 1 if offset > 0 else -1
        outside = lane >= LANES - offset if offset > 0 else lane < -offset
        shifts.append(
            [
                jnp.where(outside, turned[t + step] if 0 <= t + step < count else 0.0, turned[t])
                for t in range(count)
            ]
        )
    return [tuple(s[t] for s in shifts) for t in range(count)]


def plane_update(part, coef, base):
    k8, k1 = SECTION_STEP * 8.0 / 12.0, SECTION_STEP / 12.0
    r1, r2 = SECTION_STEP * VISCOSITY * 16.0 / 12.0, SECTION_STEP * VISCOSITY / 12.0
    c0 = -3.0 * 30.0 / 12.0 * SECTION_STEP * VISCOSITY

    def slope(far, near, p1, m1, p2, m2):
        return near * (p1 - m1) - far * (p2 - m2)

    totals = {}
    extra = {}
    for var in (4, 2, 3, 1, 0):
        centre = part(var, 0, 0)
        axial = axial_shifts(centre)
        cycle = list(zip(*[part(var, d, 0) for d in (1, -1, 2, -2)]))
        band = list(zip(*[part(var, 0, d) for d in (1, -1, 2, -2)]))
        values = base(var)
        totals[var] = []
        for t, x in enumerate(centre):
            total = values[t] + c0 * x
            for i in range(4):
                total += coef(i) * cycle[t][i]
                total += coef(7 + i) * axial[t][i]
            total += r1 * (band[t][0] + band[t][1])
            total -= r2 * (band[t][2] + band[t][3])
            if var == 4:
                extra[1, t] = slope(coef(5), coef(4), *cycle[t])
                extra[2, t] = slope(k1, k8, *band[t])
                extra[3, t] = slope(k1, k8, *axial[t])
            elif var == 2:
                extra[0, t] = slope(k1, k8, *band[t]) + coef(6) * x
            elif var == 3:
                extra[0, t] += slope(k1, k8, *axial[t])
            elif var == 1:
                extra[0, t] += slope(coef(5), coef(4), *cycle[t])
            if var in (1, 2, 3, 0):
                total -= extra[var, t]
            totals[var].append(total)
    for t in range(len(totals[4])):
        totals[4][t] -= extra[0, t]
    return totals


def pack_kernel(flow_ref, *refs, rad, with_az):
    *outs, edge_ref, sems = refs
    rad_first_ref, rad_last_ref = outs[-2:]
    planes, rows = flow_ref.shape[1:3]
    direct, edges = [], []
    for s, var in enumerate(rad):
        for side, start in enumerate((0, rows - EDGE)):
            edges.append(
                pltpu.make_async_copy(
                    flow_ref.at[var, :, pl.ds(start, EDGE)],
                    edge_ref.at[side, s],
                    sems.at[side, s],
                )
            )
    if with_az:
        for side, (ref, start) in enumerate(zip(outs, (0, planes - 2))):
            direct.append(
                pltpu.make_async_copy(
                    flow_ref.at[:, pl.ds(start, 2)], ref, sems.at[side, len(rad)]
                )
            )
    for c in edges + direct:
        c.start()
    for c in edges:
        c.wait()
    for a in range(planes):
        for s in range(len(rad)):
            rad_first_ref[a, 2 * s : 2 * s + 2, :] = edge_ref[0, s, a, 0:2, :]
            rad_last_ref[a, 2 * s : 2 * s + 2, :] = edge_ref[1, s, a, EDGE - 2 : EDGE, :]
    for c in direct:
        c.wait()


def fill_coefficients(coef_ref, mean_ref, planes):
    rows = coef_ref.shape[1]
    dt, nu = SECTION_STEP, VISCOSITY
    eye = lax.broadcasted_iota(jnp.int32, (rows, rows), 0) == lax.broadcasted_iota(
        jnp.int32, (rows, rows), 1
    )

    def column(i):
        spread = jnp.where(eye, mean_ref[i : i + 1, :], 0.0)
        return jnp.broadcast_to(jnp.sum(spread, axis=1, keepdims=True), (rows, LANES))

    cell = lax.broadcasted_iota(jnp.int32, (rows, LANES), 0) + lax.axis_index("radius") * rows
    radius_pos = cell.astype(jnp.float32) + (0.5 * rows * lax.axis_size("radius") + 0.5)
    metric = planes * lax.axis_size("azimuth") / (2.0 * math.pi) / radius_pos
    turn = column(0) * metric
    for at, speed in ((0, turn), (7, column(1))):
        coef_ref[at] = dt * (nu * 16.0 / 12.0 - speed * (8.0 / 12.0))
        coef_ref[at + 1] = dt * (nu * 16.0 / 12.0 + speed * (8.0 / 12.0))
        coef_ref[at + 2] = dt * (speed / 12.0 - nu / 12.0)
        coef_ref[at + 3] = -dt * (speed / 12.0 + nu / 12.0)
    coef_ref[4] = dt * 8.0 / 12.0 * metric
    coef_ref[5] = dt / 12.0 * metric
    coef_ref[6] = dt / radius_pos


def panels_kernel(
    owner_ref,
    count_ref,
    line_ref,
    mean_ref,
    order_ref,
    flow_ref,
    base_ref,
    history_ref,
    out_ref,
    rows_ref,
    coef_ref,
    mask_ref,
    slots_ref,
    store_ref,
    wide_ref,
    block_ref,
    rank_ref,
    own_ref,
    sems,
):
    planes, tiles, band = store_ref.shape[1:4]
    sources = ((flow_ref, 4), (flow_ref, 1), (flow_ref, 2), (flow_ref, 3), (base_ref, 4))
    copies = [
        pltpu.make_async_copy(
            ref.at[var, :, :, pl.ds(t * LANES, LANES)], store_ref.at[s, :, t], sems.at[s, t]
        )
        for s, (ref, var) in enumerate(sources)
        for t in range(tiles)
    ]
    cycle, radius = lax.axis_index("azimuth"), lax.axis_index("radius")
    owners = pltpu.make_async_copy(owner_ref.at[cycle], own_ref, sems.at[len(sources), 0])
    owners.start()
    for c in copies:
        c.start()
    mine = order_ref[cycle * lax.axis_size("radius") + radius]
    block = lax.broadcasted_iota(jnp.int32, mask_ref.shape, 1)
    mask_ref[...] = jnp.where(block == mine, 1.0, 0.0)
    count = count_ref[radius, cycle]
    slots_ref[2 * KMAX] = count
    fill_coefficients(coef_ref, mean_ref, planes)
    wide_ref[ROWS - 1] = jnp.zeros_like(wide_ref[ROWS - 1])
    for r in range(ROWS):
        width = min(LANES, history_ref.shape[1] - r * LANES)
        chunk = history_ref[:, r * LANES : r * LANES + width]
        wide_ref[r, :, 0:width] = chunk.astype(jnp.float32)
    out_ref[...] = jnp.zeros_like(out_ref)

    for q in range(rank_ref.shape[0]):
        rank_ref[q] = 0
    owners.wait()

    def place(k, carry):
        owner = own_ref[radius, k]
        rank = rank_ref[owner]
        rank_ref[owner] = rank + 1
        slots_ref[k] = owner
        slots_ref[KMAX + k] = rank
        for r in range(ROWS):
            block_ref[r : r + 1, :] = wide_ref[r, pl.ds(k, 1), :]
        at = pl.ds(pl.multiple_of(rank * ROWS, ROWS), ROWS)
        out_ref[owner, at, :] = block_ref[...].astype(out_ref.dtype)
        return carry

    lax.fori_loop(0, count, place, 0)
    for c in copies:
        c.wait()

    lane = lax.broadcasted_iota(jnp.int32, (1, LANES), 1)
    k8, k1 = SECTION_STEP * 8.0 / 12.0, SECTION_STEP / 12.0
    r1, r2 = SECTION_STEP * VISCOSITY * 16.0 / 12.0, SECTION_STEP * VISCOSITY / 12.0

    def shifted(x, offset):
        turned = [pltpu.roll(t, (-offset) % LANES, 1) for t in x]
        zero = jnp.zeros_like(x[0])
        if offset < 0:
            return [
                jnp.where(lane < -offset, turned[t - 1] if t else zero, turned[t])
                for t in range(tiles)
            ]
        return [
            jnp.where(lane >= LANES - offset, turned[t + 1] if t + 1 < tiles else zero, turned[t])
            for t in range(tiles)
        ]

    def local(k, carry):
        line = line_ref[0, 0, k]
        la, lr = lax.div(line, band), lax.rem(line, band)

        def row(s, a, r):
            return [store_ref[s, a, t, pl.ds(r, 1), :] for t in range(tiles)]

        def coef(i, inside=None):
            value = coef_ref[i, pl.ds(lr, 1), :]
            return value if inside is None else jnp.where(inside, value, 0.0)

        center = row(0, la, lr)
        total = row(4, la, lr)

        def add(share, x):
            for t in range(tiles):
                total[t] = total[t] + share * x[t]

        add(-3.0 * 30.0 / 12.0 * SECTION_STEP * VISCOSITY, center)
        add(-coef(6), row(2, la, lr))
        turn = {1: -1.0, -1: 1.0, 2: 1.0, -2: -1.0}
        wind = row(3, la, lr)
        for i, offset in enumerate((1, -1, 2, -2)):
            far = abs(offset) == 2
            plane = la + offset
            inside = jnp.logical_and(plane >= 0, plane < planes)
            plane = jnp.clip(plane, 0, planes - 1)
            add(coef(i, inside), row(0, plane, lr))
            add(turn[offset] * coef(5 if far else 4, inside), row(1, plane, lr))
            cell = lr + offset
            inside = jnp.logical_and(cell >= 0, cell < band)
            cell = jnp.clip(cell, 0, band - 1)
            add(jnp.where(inside, -r2 if far else r1, 0.0), row(0, la, cell))
            add(jnp.where(inside, turn[offset] * (k1 if far else k8), 0.0), row(2, la, cell))
            add(coef(7 + i), shifted(center, offset))
            add(turn[offset] * (k1 if far else k8), shifted(wind, offset))
        for t in range(tiles):
            rows_ref[k, t : t + 1, :] = total[t]
        return carry

    lax.fori_loop(0, count, local, 0)


def fresh_kernel(
    slots_ref,
    line_ref,
    start_ref,
    coef_ref,
    rows_ref,
    before_ref,
    after_ref,
    lo_ref,
    hi_ref,
    held_ref,
    out_ref,
    ring_ref,
    sum_ref,
    sems,
):
    tiles, band = ring_ref.shape[1:3]
    planes = lo_ref.shape[0]
    copies = []
    for s, var in enumerate((1, 4)):
        for side, ref in enumerate((before_ref, after_ref)):
            for t in range(tiles):
                src = ref.at[var, :, :, pl.ds(t * LANES, LANES)]
                dst = ring_ref.at[pl.ds(4 * s + 2 * side, 2), t]
                copies.append(pltpu.make_async_copy(src, dst, sems.at[s, side, t]))
    for c in copies:
        c.start()
    out_ref[...] = held_ref[...]
    lane = lax.broadcasted_iota(jnp.int32, (ROWS, LANES), 1)
    row_of = lax.broadcasted_iota(jnp.int32, (ROWS, LANES), 0)
    k8, k1 = SECTION_STEP * 8.0 / 12.0, SECTION_STEP / 12.0
    r1, r2 = SECTION_STEP * VISCOSITY * 16.0 / 12.0, SECTION_STEP * VISCOSITY / 12.0

    def shares(spot, count, near_before, far_before, near_after, far_after):
        first, second = spot == 0, spot == 1
        last, other = spot == count - 1, spot == count - 2
        return (
            jnp.where(first, far_before, 0.0),
            jnp.where(first, near_before, jnp.where(second, far_before, 0.0)),
            jnp.where(last, near_after, jnp.where(other, far_after, 0.0)),
            jnp.where(last, far_after, 0.0),
        )

    def put(k, carry):
        owner, rank = slots_ref[k], slots_ref[KMAX + k]
        line, start = line_ref[0, 0, k], start_ref[0, 0, k]
        la, lr = lax.div(line, band), lax.rem(line, band)
        for t in range(tiles):
            sum_ref[t : t + 1, :] = rows_ref[k, t : t + 1, :]

        @pl.when(jnp.logical_or(la < 2, la >= planes - 2))
        def _():
            c = [coef_ref[i, pl.ds(lr, 1), :] for i in range(6)]
            wind = shares(la, planes, c[4], -c[5], -c[4], c[5])
            own = shares(la, planes, c[1], c[3], c[0], c[2])
            for t in range(tiles):
                total = sum_ref[t : t + 1, :]
                for j in range(4):
                    total += wind[j] * ring_ref[j, t, pl.ds(lr, 1), :]
                    total += own[j] * ring_ref[4 + j, t, pl.ds(lr, 1), :]
                sum_ref[t : t + 1, :] = total

        @pl.when(jnp.logical_or(lr < 2, lr >= band - 2))
        def _():
            wind = shares(lr, band, k8, -k1, -k8, k1)
            own = shares(lr, band, r1, -r2, r1, -r2)
            for t in range(tiles):
                at = slice(t * LANES, (t + 1) * LANES)
                total = sum_ref[t : t + 1, :]
                for j in range(4):
                    ref = lo_ref if j < 2 else hi_ref
                    total += wind[j] * ref[la, j % 2 : j % 2 + 1, at]
                    total += own[j] * ref[la, 2 + j % 2 : 3 + j % 2, at]
                sum_ref[t : t + 1, :] = total

        tile, off = lax.div(start, LANES), lax.rem(start, LANES)
        other = jnp.minimum(tile + 1, tiles - 1)
        shift = lax.rem(2 * LANES - BP - off, LANES)
        x0 = jnp.broadcast_to(sum_ref[pl.ds(tile, 1), :], (ROWS, LANES))
        x1 = jnp.broadcast_to(sum_ref[pl.ds(other, 1), :], (ROWS, LANES))
        window = jnp.where(
            lane < 2 * LANES - BP - off, pltpu.roll(x0, shift, 1), pltpu.roll(x1, shift, 1)
        )
        at = pl.ds(pl.multiple_of(rank * ROWS, ROWS), ROWS)
        block = out_ref[owner, at, :].astype(jnp.float32)
        place = jnp.logical_and(row_of == ROWS - 1, lane >= LANES - BP)
        out_ref[owner, at, :] = jnp.where(place, window, block).astype(out_ref.dtype)
        return carry

    for c in copies:
        c.wait()
    lax.fori_loop(0, slots_ref[2 * KMAX], put, 0)


def fields_kernel(
    flow_ref,
    before_ref,
    after_ref,
    base_ref,
    lo0_ref,
    hi0_ref,
    lo1_ref,
    hi1_ref,
    coef_ref,
    next_ref,
    ext_ref,
    sems,
):
    group = pl.program_id(0)
    planes, rows, length = flow_ref.shape[1:]
    tiles = length // LANES
    stages = plane_copies(flow_ref, before_ref, after_ref, ext_ref, sems)

    def radial_layers(plane, carry):
        for var in range(NVAR):
            if var in FIRST_RAD:
                lo, hi, s = lo0_ref, hi0_ref, FIRST_RAD.index(var)
            else:
                lo, hi, s = lo1_ref, hi1_ref, LATER_RAD.index(var)
            for t in range(tiles):
                at = slice(2 * s, 2 * s + 2), slice(t * LANES, (t + 1) * LANES)
                ext_ref[var, plane + 2, t, EDGE - 2 : EDGE, :] = lo[(plane, *at)]
                ext_ref[var, plane + 2, t, EDGE + rows : EDGE + rows + 2, :] = hi[(plane, *at)]
        return carry

    @pl.when(group == 0)
    def _():
        for stage in stages:
            for c in stage:
                c.start()
        lax.fori_loop(0, planes, radial_layers, 0)
        for c in stages[0] + stages[1]:
            c.wait()

    def one(inner, carry):
        a = group * CHUNK + inner
        for i, stage in enumerate(stages[2:]):

            @pl.when(a == (i + 1) * CHUNK - 2)
            def _():
                for c in stage:
                    c.wait()

        half = 8
        for start in range(0, rows, half):
            at = slice(start, start + half)

            def part(var, offset, row_shift):
                first = EDGE + start + row_shift
                return [
                    ext_ref[var, a + 2 + offset, t, first : first + half, :] for t in range(tiles)
                ]

            held = [coef_ref[i, at, :] for i in range(coef_ref.shape[0])]

            def base(var):
                return [
                    base_ref[var, inner, at, t * LANES : (t + 1) * LANES] for t in range(tiles)
                ]

            totals = plane_update(part, held.__getitem__, base)
            for var in range(NVAR):
                for t in range(tiles):
                    next_ref[var, inner, at, t * LANES : (t + 1) * LANES] = totals[var][t]
        return carry

    lax.fori_loop(0, CHUNK, one, 0)


ANY = pl.BlockSpec(memory_space=pltpu.HBM)
IN_SMEM = pl.BlockSpec(memory_space=pltpu.SMEM)
IN_VMEM = pl.BlockSpec(memory_space=pltpu.VMEM)
MIB = 1 << 20


def limits(mib, **more):
    return pltpu.CompilerParams(vmem_limit_bytes=mib * MIB, **more)


def cost(flops, moved):
    return pl.CostEstimate(flops=flops, bytes_accessed=moved, transcendentals=0)


def in_hbm(array):
    return pltpu.with_memory_space_constraint(array, pltpu.HBM)


def whole(array):
    shape = array.shape
    return pl.BlockSpec(shape, lambda *_: (0,) * len(shape))


def pack_call(flow, rad, with_az):
    nvar, planes, rows, length = flow.shape
    az_shape = jax.ShapeDtypeStruct((nvar, 2, rows, length), jnp.float32)
    rad_shape = jax.ShapeDtypeStruct((planes, 2 * len(rad), length), jnp.float32)
    shapes = (az_shape,) * (2 * with_az) + (rad_shape,) * 2
    return pl.pallas_call(
        functools.partial(pack_kernel, rad=rad, with_az=with_az),
        out_shape=shapes,
        in_specs=[ANY],
        out_specs=(IN_VMEM,) * len(shapes),
        scratch_shapes=[
            pltpu.VMEM((2, len(rad), planes, EDGE, length), jnp.float32),
            pltpu.SemaphoreType.DMA((2, len(rad) + 1)),
        ],
        compiler_params=limits(8),
        cost_estimate=cost(0, 20 * MIB),
    )(in_hbm(flow))


def panels_call(owner, count, line, mean_flow, order, flow, base, history):
    _, planes, rows, length = flow.shape
    owners, tiles = count.shape[1], length // LANES
    return pl.pallas_call(
        panels_kernel,
        name="panels",
        out_shape=(
            jax.ShapeDtypeStruct((owners, CAP * ROWS, LANES), jnp.bfloat16),
            jax.ShapeDtypeStruct((KMAX, 8, LANES), jnp.float32),
            jax.ShapeDtypeStruct((11, rows, LANES), jnp.float32),
            jax.ShapeDtypeStruct((1, order.shape[0]), jnp.float32),
            jax.ShapeDtypeStruct((LANES,), jnp.int32),
        ),
        in_specs=[ANY, IN_SMEM, IN_SMEM, IN_VMEM, IN_SMEM, ANY, ANY, IN_VMEM],
        out_specs=(IN_VMEM,) * 4 + (IN_SMEM,),
        scratch_shapes=[
            pltpu.VMEM((5, planes, tiles, rows, LANES), jnp.float32),
            pltpu.VMEM((ROWS, KMAX, LANES), jnp.float32),
            pltpu.VMEM((ROWS, LANES), jnp.float32),
            pltpu.SMEM((owners,), jnp.int32),
            pltpu.SMEM(owner.shape[1:], jnp.int32),
            pltpu.SemaphoreType.DMA((6, tiles)),
        ],
        compiler_params=limits(8),
        cost_estimate=cost(0, 5 * 4 * planes * rows * length),
    )(in_hbm(owner), count, line, mean_flow, order, in_hbm(flow), in_hbm(base), history)


def fresh_call(slots, line, start, coef, rows, az, rad, held):
    length = az[0].shape[-1]
    band = az[0].shape[2]
    return pl.pallas_call(
        fresh_kernel,
        name="fresh",
        out_shape=jax.ShapeDtypeStruct(held.shape, held.dtype),
        in_specs=[IN_SMEM] * 3 + [IN_VMEM] * 2 + [pl.BlockSpec(memory_space=pl.ANY)] * 2 + [IN_VMEM] * 3,
        out_specs=IN_VMEM,
        scratch_shapes=[
            pltpu.VMEM((8, length // LANES, band, LANES), jnp.float32),
            pltpu.VMEM((8, LANES), jnp.float32),
            pltpu.SemaphoreType.DMA((2, 2, length // LANES)),
        ],
        compiler_params=limits(8),
        cost_estimate=cost(0, 4 * 4 * band * length * 4),
    )(slots, line, start, coef, rows, *az, *rad, held)


def fields_call(flow, az, base, rad0, rad1, coef):
    nvar, planes, rows, length = flow.shape
    cells = planes * rows * length
    every = (nvar, CHUNK, rows, length)
    args = (in_hbm(flow), *az, in_hbm(base), *rad0, *rad1, coef)
    return pl.pallas_call(
        fields_kernel,
        name="fields",
        out_shape=jax.ShapeDtypeStruct(flow.shape, jnp.float32),
        grid=(planes // CHUNK,),
        in_specs=[
            *[ANY] + [pl.BlockSpec(memory_space=pl.ANY)] * 2,
            pl.BlockSpec(every, lambda a: (0, a, 0, 0)),
            *[whole(x) for x in (*rad0, *rad1, coef)],
        ],
        out_specs=pl.BlockSpec(every, lambda a: (0, a, 0, 0)),
        scratch_shapes=[
            pltpu.VMEM(
                (nvar, planes + 4, length // LANES, rows + 2 * EDGE, LANES), jnp.float32
            ),
            pltpu.SemaphoreType.DMA((planes // CHUNK + 2, nvar, length // LANES)),
        ],
        compiler_params=limits(18, dimension_semantics=("arbitrary",)),
        cost_estimate=cost(250 * cells, 15 * 4 * cells),
    )(*args)


def weights_kernel(
    stations_ref,
    order_ref,
    weight_ref,
    out_ref,
    lhs_ref,
    held_ref,
    order_held_ref,
    spot_ref,
    sems,
):
    chunks, _, width = held_ref.shape
    copies = [
        pltpu.make_async_copy(
            weight_ref.at[:, pl.ds(i * width, width)], held_ref.at[i], sems.at[i]
        )
        for i in range(chunks)
    ]
    orders = pltpu.make_async_copy(order_ref, order_held_ref, sems.at[chunks])
    orders.start()
    for c in copies:
        c.start()
    for group in range(stations_ref.shape[0] * CAP // QUADS):
        tiles = []
        for m in range(QUADS):
            source, rank = divmod(group * QUADS + m, CAP)
            tile = stations_ref[source, rank * ROWS : (rank + 1) * ROWS, :]
            tiles.append(tile.astype(jnp.float32))
        for i, tile in enumerate(swap_quads(tiles)):
            lhs_ref[i * ROWS : (i + 1) * ROWS, group * LANES : (group + 1) * LANES] = tile.astype(
                lhs_ref.dtype
            )

    def place(j, carry):
        spot_ref[order_held_ref[j]] = j
        return carry

    orders.wait()
    lax.fori_loop(0, out_ref.shape[0], place, 0, unroll=8)
    groups = width // LANES
    for n, c in enumerate(copies):
        c.wait()
        part = jnp.dot(lhs_ref[...], held_ref[n], preferred_element_type=jnp.float32)
        for group in range(groups):
            lanes = slice(group * LANES, (group + 1) * LANES)
            tiles = [part[i * ROWS : (i + 1) * ROWS, lanes] for i in range(QUADS)]
            for m, tile in enumerate(swap_quads(tiles)):
                out_ref[spot_ref[(n * groups + group) * QUADS + m]] = tile


def weights_call(order, stations, weight):
    count = order.shape[0]
    depth, observers = weight.shape
    chunks = observers // WIDTH
    return pl.pallas_call(
        weights_kernel,
        name="observers",
        out_shape=jax.ShapeDtypeStruct((count, ROWS, LANES), jnp.float32),
        in_specs=[IN_VMEM, ANY, ANY],
        out_specs=IN_VMEM,
        scratch_shapes=[
            pltpu.VMEM((NT, depth), jnp.bfloat16),
            pltpu.VMEM((chunks, depth, WIDTH), jnp.bfloat16),
            pltpu.SMEM((count,), jnp.int32),
            pltpu.SMEM((count,), jnp.int32),
            pltpu.SemaphoreType.DMA((chunks + 1,)),
        ],
        compiler_params=limits(14),
        cost_estimate=cost(2 * NT * depth * observers, 2 * depth * observers),
    )(stations, in_hbm(order), in_hbm(weight))


def retard_kernel(total_ref, matrix_ref, out_ref, times_ref, late_ref):
    total = total_ref[...]
    for i in range(QUADS):
        turned = total if i == 0 else pltpu.roll(total, LANES - i * BP, 1)
        times_ref[pl.ds(i, ROWS, stride=QUADS), :] = turned
    late_ref[...] = jnp.dot(
        matrix_ref[...],
        times_ref[...],
        precision=lax.Precision.HIGHEST,
        preferred_element_type=jnp.float32,
    )
    lane = lax.broadcasted_iota(jnp.int32, (ROWS, LANES), 1)
    out = late_ref[pl.ds(0, ROWS, stride=QUADS), :]
    for i in range(1, QUADS):
        tile = pltpu.roll(late_ref[pl.ds(i, ROWS, stride=QUADS), :], i * BP, 1)
        out = jnp.where(lane >= i * BP, tile, out)
    out_ref[...] = out


def retard_call(total, matrix):
    return pl.pallas_call(
        retard_kernel,
        name="retard",
        out_shape=jax.ShapeDtypeStruct((ROWS, LANES), jnp.float32),
        in_specs=[pl.BlockSpec(memory_space=pltpu.VMEM)] * 2,
        out_specs=pl.BlockSpec(memory_space=pltpu.VMEM),
        scratch_shapes=[pltpu.VMEM((NT, LANES), jnp.float32)] * 2,
        compiler_params=limits(4),
        cost_estimate=cost(2 * NT * NT * LANES, 4 * NT * NT),
    )(total, matrix)


def exchange(first, last, axis, wrap):
    count = lax.axis_size(axis)
    up = [(i, (i + 1) % count) for i in range(count if wrap else count - 1)]
    down = [(j, i) for i, j in up]
    return lax.ppermute(last, axis, up), lax.ppermute(first, axis, down)


def per_device(
    flow_state,
    base_state,
    mean_flow,
    panel_history,
    panel_line,
    panel_start,
    panel_count,
    panel_owner,
    source_weight,
    retarded_time,
    observer_block,
):
    az_first, az_last, *ends = pack_call(flow_state, FIRST_RAD, True)
    az = exchange(az_first, az_last, "azimuth", True)
    rad0 = exchange(*ends, "radius", False)
    history, local, coef, mask, slots = panels_call(
        panel_owner,
        panel_count.T,
        panel_line,
        mean_flow,
        observer_block,
        flow_state,
        base_state,
        panel_history[0, 0],
    )
    outgoing = fresh_call(slots, panel_line, panel_start, coef, local, az, rad0, history)
    stations = lax.all_to_all(outgoing, "azimuth", split_axis=0, concat_axis=0, tiled=True)
    later, _ = lax.optimization_barrier((flow_state, outgoing))
    packed = pack_call(later, LATER_RAD, False)
    rad1 = exchange(*packed, "radius", False)
    times, _ = lax.optimization_barrier((retarded_time, outgoing))
    matrix = jnp.sum(times * mask[0][:, None, None], axis=0)
    sends = weights_call(observer_block, stations, source_weight[0])
    sends = (WIRE_SCALE * sends).astype(jnp.float16)
    parts = lax.all_to_all(sends, BOTH, split_axis=0, concat_axis=0, tiled=True)
    next_state = fields_call(flow_state, az, base_state, rad0, rad1, coef)

    total = (1.0 / WIRE_SCALE) * jnp.sum(parts.astype(jnp.float32), axis=0)
    pressure = retard_call(total, matrix)
    return next_state, pressure.reshape(1, ROWS * LANES)


def solution(mesh):
    placed = (
        P(None, "azimuth", "radius", None),
        P(None, "azimuth", "radius", None),
        P(None, "radius"),
        P("azimuth", "radius", None, None),
        P("azimuth", "radius", None),
        P("azimuth", "radius", None),
        P(),
        P(),
        P("radius", "azimuth", None),
        P(),
        P(),
    )

    return jax.shard_map(
        per_device,
        mesh=mesh,
        in_specs=placed,
        out_specs=(P(None, "azimuth", "radius", None), P(BOTH, None)),
        check_vma=False,
    )
```

```python
import math

import jax
import jax.numpy as jnp
from jax import lax
from jax.experimental import pallas as pl
from jax.experimental.pallas import tpu as pltpu
from jax.sharding import PartitionSpec as P

NT = 64
BP = 32
KMAX = 16
CAP = 2
LANES = 128
ROWS = NT * BP // LANES
QUADS = LANES // BP
WIRE_SCALE = 64.0
WIDTH = 1024

SECTION_STEP = 0.3
VISCOSITY = 0.05
BOTH = ("azimuth", "radius")

NVAR = 5
FIRST_RAD = (2, 4)
LATER_RAD = (0, 1, 3)


def swap_quads(tiles):
    lane = lax.broadcasted_iota(jnp.int32, tiles[0].shape, 1)
    low, even = (lane % 128) < 64, (lane % 64) < 32
    a0, a1, a2, a3 = tiles

    def turn(x, shift):
        return pltpu.roll(x, shift, 1)

    b0 = jnp.where(low, a0, turn(a2, 64))
    b2 = jnp.where(low, turn(a0, 64), a2)
    b1 = jnp.where(low, a1, turn(a3, 64))
    b3 = jnp.where(low, turn(a1, 64), a3)
    return (
        jnp.where(even, b0, turn(b1, 32)),
        jnp.where(even, turn(b0, 96), b1),
        jnp.where(even, b2, turn(b3, 32)),
        jnp.where(even, turn(b2, 96), b3),
    )


EDGE = 8
CHUNK = 4


def plane_copies(flow_ref, before_ref, after_ref, ext_ref, sems):
    planes, rows, length = flow_ref.shape[1:]
    sources = [(before_ref, 0, 0, 2)]
    for first in range(0, planes, CHUNK):
        sources.append((flow_ref, first, first + 2, CHUNK))
    sources.append((after_ref, 0, planes + 2, 2))
    stages = []
    for stage, (ref, first, spot, count) in enumerate(sources):
        stages.append([])
        for var in range(NVAR):
            for t in range(length // LANES):
                src = ref.at[var, pl.ds(first, count), :, pl.ds(t * LANES, LANES)]
                dst = ext_ref.at[var, pl.ds(spot, count), t, pl.ds(EDGE, rows)]
                stages[-1].append(pltpu.make_async_copy(src, dst, sems.at[stage, var, t]))
    return stages


def axial_shifts(tiles):
    lane = lax.broadcasted_iota(jnp.int32, tiles[0].shape, 1)
    count = len(tiles)
    shifts = []
    for offset in (1, -1, 2, -2):
        turned = [pltpu.roll(t, (-offset) % LANES, 1) for t in tiles]
        step = 1 if offset > 0 else -1
        outside = lane >= LANES - offset if offset > 0 else lane < -offset
        shifts.append(
            [
                jnp.where(outside, turned[t + step] if 0 <= t + step < count else 0.0, turned[t])
                for t in range(count)
            ]
        )
    return [tuple(s[t] for s in shifts) for t in range(count)]


def plane_update(part, coef, base):
    k8, k1 = SECTION_STEP * 8.0 / 12.0, SECTION_STEP / 12.0
    r1, r2 = SECTION_STEP * VISCOSITY * 16.0 / 12.0, SECTION_STEP * VISCOSITY / 12.0
    c0 = -3.0 * 30.0 / 12.0 * SECTION_STEP * VISCOSITY

    def slope(far, near, p1, m1, p2, m2):
        return near * (p1 - m1) - far * (p2 - m2)

    totals = {}
    extra = {}
    for var in (4, 2, 3, 1, 0):
        centre = part(var, 0, 0)
        axial = axial_shifts(centre)
        cycle = list(zip(*[part(var, d, 0) for d in (1, -1, 2, -2)]))
        band = list(zip(*[part(var, 0, d) for d in (1, -1, 2, -2)]))
        values = base(var)
        totals[var] = []
        for t, x in enumerate(centre):
            total = values[t] + c0 * x
            for i in range(4):
                total += coef(i) * cycle[t][i]
                total += coef(7 + i) * axial[t][i]
            total += r1 * (band[t][0] + band[t][1])
            total -= r2 * (band[t][2] + band[t][3])
            if var == 4:
                extra[1, t] = slope(coef(5), coef(4), *cycle[t])
                extra[2, t] = slope(k1, k8, *band[t])
                extra[3, t] = slope(k1, k8, *axial[t])
            elif var == 2:
                extra[0, t] = slope(k1, k8, *band[t]) + coef(6) * x
            elif var == 3:
                extra[0, t] += slope(k1, k8, *axial[t])
            elif var == 1:
                extra[0, t] += slope(coef(5), coef(4), *cycle[t])
            if var in (1, 2, 3, 0):
                total -= extra[var, t]
            totals[var].append(total)
    for t in range(len(totals[4])):
        totals[4][t] -= extra[0, t]
    return totals


def edge_copies(flow_ref, edge_ref, sems, rad):
    copies = []
    for s, var in enumerate(rad):
        for side, start in enumerate((0, flow_ref.shape[2] - EDGE)):
            src = flow_ref.at[var, :, pl.ds(start, EDGE)]
            copies.append(pltpu.make_async_copy(src, edge_ref.at[side, s], sems.at[side, s]))
    return copies


def place_edges(edge_ref, first_ref, last_ref):
    for a in range(edge_ref.shape[2]):
        for s in range(edge_ref.shape[1]):
            first_ref[a, 2 * s : 2 * s + 2, :] = edge_ref[0, s, a, 0:2, :]
            last_ref[a, 2 * s : 2 * s + 2, :] = edge_ref[1, s, a, EDGE - 2 : EDGE, :]


def pack_kernel(
    flow_ref, az_first_ref, az_last_ref, rad_first_ref, rad_last_ref, edge_ref, sems, az_sems
):
    planes = flow_ref.shape[1]
    edges = edge_copies(flow_ref, edge_ref, sems, FIRST_RAD)
    direct = [
        pltpu.make_async_copy(flow_ref.at[:, pl.ds(start, 2)], ref, az_sems.at[side])
        for side, (ref, start) in enumerate(((az_first_ref, 0), (az_last_ref, planes - 2)))
    ]
    for c in edges + direct:
        c.start()
    for c in edges:
        c.wait()
    place_edges(edge_ref, rad_first_ref, rad_last_ref)
    for c in direct:
        c.wait()


def fill_coefficients(coef_ref, mean_ref, planes):
    rows = coef_ref.shape[1]
    dt, nu = SECTION_STEP, VISCOSITY
    eye = lax.broadcasted_iota(jnp.int32, (rows, rows), 0) == lax.broadcasted_iota(
        jnp.int32, (rows, rows), 1
    )

    def column(i):
        spread = jnp.where(eye, mean_ref[i : i + 1, :], 0.0)
        return jnp.broadcast_to(jnp.sum(spread, axis=1, keepdims=True), (rows, LANES))

    cell = lax.broadcasted_iota(jnp.int32, (rows, LANES), 0) + lax.axis_index("radius") * rows
    radius_pos = cell.astype(jnp.float32) + (0.5 * rows * lax.axis_size("radius") + 0.5)
    metric = planes * lax.axis_size("azimuth") / (2.0 * math.pi) / radius_pos
    turn = column(0) * metric
    for at, speed in ((0, turn), (7, column(1))):
        coef_ref[at] = dt * (nu * 16.0 / 12.0 - speed * (8.0 / 12.0))
        coef_ref[at + 1] = dt * (nu * 16.0 / 12.0 + speed * (8.0 / 12.0))
        coef_ref[at + 2] = dt * (speed / 12.0 - nu / 12.0)
        coef_ref[at + 3] = -dt * (speed / 12.0 + nu / 12.0)
    coef_ref[4] = dt * 8.0 / 12.0 * metric
    coef_ref[5] = dt / 12.0 * metric
    coef_ref[6] = dt / radius_pos


def panels_kernel(
    owner_ref,
    count_ref,
    line_ref,
    mean_ref,
    order_ref,
    flow_ref,
    base_ref,
    history_ref,
    out_ref,
    rows_ref,
    coef_ref,
    mask_ref,
    first_ref,
    last_ref,
    slots_ref,
    store_ref,
    wide_ref,
    block_ref,
    edge_ref,
    rank_ref,
    own_ref,
    sems,
    edge_sems,
):
    planes, tiles, band = store_ref.shape[1:4]
    sources = ((flow_ref, 4), (flow_ref, 1), (flow_ref, 2), (flow_ref, 3), (base_ref, 4))
    copies = [
        pltpu.make_async_copy(
            ref.at[var, :, :, pl.ds(t * LANES, LANES)], store_ref.at[s, :, t], sems.at[s, t]
        )
        for s, (ref, var) in enumerate(sources)
        for t in range(tiles)
    ]
    cycle, radius = lax.axis_index("azimuth"), lax.axis_index("radius")
    owners = pltpu.make_async_copy(owner_ref.at[cycle], own_ref, sems.at[len(sources), 0])
    owners.start()
    edges = edge_copies(flow_ref, edge_ref, edge_sems, LATER_RAD)
    for c in copies + edges:
        c.start()
    mine = order_ref[cycle * lax.axis_size("radius") + radius]
    block = lax.broadcasted_iota(jnp.int32, mask_ref.shape, 1)
    mask_ref[...] = jnp.where(block == mine, 1.0, 0.0)
    count = count_ref[radius, cycle]
    slots_ref[2 * KMAX] = count
    fill_coefficients(coef_ref, mean_ref, planes)
    wide_ref[ROWS - 1] = jnp.zeros_like(wide_ref[ROWS - 1])
    for r in range(ROWS):
        width = min(LANES, history_ref.shape[1] - r * LANES)
        chunk = history_ref[:, r * LANES : r * LANES + width]
        wide_ref[r, :, 0:width] = chunk.astype(jnp.float32)
    out_ref[...] = jnp.zeros_like(out_ref)

    for q in range(rank_ref.shape[0]):
        rank_ref[q] = 0
    owners.wait()

    def place(k, carry):
        owner = own_ref[radius, k]
        rank = rank_ref[owner]
        rank_ref[owner] = rank + 1
        slots_ref[k] = owner
        slots_ref[KMAX + k] = rank
        for r in range(ROWS):
            block_ref[r : r + 1, :] = wide_ref[r, pl.ds(k, 1), :]
        at = pl.ds(pl.multiple_of(rank * ROWS, ROWS), ROWS)
        out_ref[owner, at, :] = block_ref[...].astype(out_ref.dtype)
        return carry

    lax.fori_loop(0, count, place, 0)
    for c in copies:
        c.wait()

    lane = lax.broadcasted_iota(jnp.int32, (1, LANES), 1)
    k8, k1 = SECTION_STEP * 8.0 / 12.0, SECTION_STEP / 12.0
    r1, r2 = SECTION_STEP * VISCOSITY * 16.0 / 12.0, SECTION_STEP * VISCOSITY / 12.0

    def shifted(x, offset):
        turned = [pltpu.roll(t, (-offset) % LANES, 1) for t in x]
        zero = jnp.zeros_like(x[0])
        if offset < 0:
            return [
                jnp.where(lane < -offset, turned[t - 1] if t else zero, turned[t])
                for t in range(tiles)
            ]
        return [
            jnp.where(lane >= LANES - offset, turned[t + 1] if t + 1 < tiles else zero, turned[t])
            for t in range(tiles)
        ]

    def local(k, carry):
        line = line_ref[0, 0, k]
        la, lr = lax.div(line, band), lax.rem(line, band)

        def row(s, a, r):
            return [store_ref[s, a, t, pl.ds(r, 1), :] for t in range(tiles)]

        def coef(i, inside=None):
            value = coef_ref[i, pl.ds(lr, 1), :]
            return value if inside is None else jnp.where(inside, value, 0.0)

        center = row(0, la, lr)
        total = row(4, la, lr)

        def add(share, x):
            for t in range(tiles):
                total[t] = total[t] + share * x[t]

        add(-3.0 * 30.0 / 12.0 * SECTION_STEP * VISCOSITY, center)
        add(-coef(6), row(2, la, lr))
        turn = {1: -1.0, -1: 1.0, 2: 1.0, -2: -1.0}
        wind = row(3, la, lr)
        for i, offset in enumerate((1, -1, 2, -2)):
            far = abs(offset) == 2
            plane = la + offset
            inside = jnp.logical_and(plane >= 0, plane < planes)
            plane = jnp.clip(plane, 0, planes - 1)
            add(coef(i, inside), row(0, plane, lr))
            add(turn[offset] * coef(5 if far else 4, inside), row(1, plane, lr))
            cell = lr + offset
            inside = jnp.logical_and(cell >= 0, cell < band)
            cell = jnp.clip(cell, 0, band - 1)
            add(jnp.where(inside, -r2 if far else r1, 0.0), row(0, la, cell))
            add(jnp.where(inside, turn[offset] * (k1 if far else k8), 0.0), row(2, la, cell))
            add(coef(7 + i), shifted(center, offset))
            add(turn[offset] * (k1 if far else k8), shifted(wind, offset))
        for t in range(tiles):
            rows_ref[k, t : t + 1, :] = total[t]
        return carry

    lax.fori_loop(0, count, local, 0)
    for c in edges:
        c.wait()
    place_edges(edge_ref, first_ref, last_ref)


def fresh_kernel(
    slots_ref,
    line_ref,
    start_ref,
    coef_ref,
    rows_ref,
    before_ref,
    after_ref,
    lo_ref,
    hi_ref,
    held_ref,
    out_ref,
    ring_ref,
    sum_ref,
    sems,
):
    tiles, band = ring_ref.shape[1:3]
    planes = lo_ref.shape[0]
    copies = []
    for s, var in enumerate((1, 4)):
        for side, ref in enumerate((before_ref, after_ref)):
            for t in range(tiles):
                src = ref.at[var, :, :, pl.ds(t * LANES, LANES)]
                dst = ring_ref.at[pl.ds(4 * s + 2 * side, 2), t]
                copies.append(pltpu.make_async_copy(src, dst, sems.at[s, side, t]))
    for c in copies:
        c.start()
    out_ref[...] = held_ref[...]
    lane = lax.broadcasted_iota(jnp.int32, (ROWS, LANES), 1)
    row_of = lax.broadcasted_iota(jnp.int32, (ROWS, LANES), 0)
    k8, k1 = SECTION_STEP * 8.0 / 12.0, SECTION_STEP / 12.0
    r1, r2 = SECTION_STEP * VISCOSITY * 16.0 / 12.0, SECTION_STEP * VISCOSITY / 12.0

    def shares(spot, count, near_before, far_before, near_after, far_after):
        first, second = spot == 0, spot == 1
        last, other = spot == count - 1, spot == count - 2
        return (
            jnp.where(first, far_before, 0.0),
            jnp.where(first, near_before, jnp.where(second, far_before, 0.0)),
            jnp.where(last, near_after, jnp.where(other, far_after, 0.0)),
            jnp.where(last, far_after, 0.0),
        )

    def put(k, carry):
        owner, rank = slots_ref[k], slots_ref[KMAX + k]
        line, start = line_ref[0, 0, k], start_ref[0, 0, k]
        la, lr = lax.div(line, band), lax.rem(line, band)
        for t in range(tiles):
            sum_ref[t : t + 1, :] = rows_ref[k, t : t + 1, :]

        @pl.when(jnp.logical_or(la < 2, la >= planes - 2))
        def _():
            c = [coef_ref[i, pl.ds(lr, 1), :] for i in range(6)]
            wind = shares(la, planes, c[4], -c[5], -c[4], c[5])
            own = shares(la, planes, c[1], c[3], c[0], c[2])
            for t in range(tiles):
                total = sum_ref[t : t + 1, :]
                for j in range(4):
                    total += wind[j] * ring_ref[j, t, pl.ds(lr, 1), :]
                    total += own[j] * ring_ref[4 + j, t, pl.ds(lr, 1), :]
                sum_ref[t : t + 1, :] = total

        @pl.when(jnp.logical_or(lr < 2, lr >= band - 2))
        def _():
            wind = shares(lr, band, k8, -k1, -k8, k1)
            own = shares(lr, band, r1, -r2, r1, -r2)
            for t in range(tiles):
                at = slice(t * LANES, (t + 1) * LANES)
                total = sum_ref[t : t + 1, :]
                for j in range(4):
                    ref = lo_ref if j < 2 else hi_ref
                    total += wind[j] * ref[la, j % 2 : j % 2 + 1, at]
                    total += own[j] * ref[la, 2 + j % 2 : 3 + j % 2, at]
                sum_ref[t : t + 1, :] = total

        tile, off = lax.div(start, LANES), lax.rem(start, LANES)
        other = jnp.minimum(tile + 1, tiles - 1)
        shift = lax.rem(2 * LANES - BP - off, LANES)
        x0 = jnp.broadcast_to(sum_ref[pl.ds(tile, 1), :], (ROWS, LANES))
        x1 = jnp.broadcast_to(sum_ref[pl.ds(other, 1), :], (ROWS, LANES))
        window = jnp.where(
            lane < 2 * LANES - BP - off, pltpu.roll(x0, shift, 1), pltpu.roll(x1, shift, 1)
        )
        at = pl.ds(pl.multiple_of(rank * ROWS, ROWS), ROWS)
        block = out_ref[owner, at, :].astype(jnp.float32)
        place = jnp.logical_and(row_of == ROWS - 1, lane >= LANES - BP)
        out_ref[owner, at, :] = jnp.where(place, window, block).astype(out_ref.dtype)
        return carry

    for c in copies:
        c.wait()
    lax.fori_loop(0, slots_ref[2 * KMAX], put, 0)


def fields_kernel(
    flow_ref,
    before_ref,
    after_ref,
    base_ref,
    lo0_ref,
    hi0_ref,
    lo1_ref,
    hi1_ref,
    coef_ref,
    next_ref,
    ext_ref,
    sems,
):
    group = pl.program_id(0)
    planes, rows, length = flow_ref.shape[1:]
    tiles = length // LANES
    stages = plane_copies(flow_ref, before_ref, after_ref, ext_ref, sems)

    def radial_layers(plane, carry):
        for var in range(NVAR):
            if var in FIRST_RAD:
                lo, hi, s = lo0_ref, hi0_ref, FIRST_RAD.index(var)
            else:
                lo, hi, s = lo1_ref, hi1_ref, LATER_RAD.index(var)
            for t in range(tiles):
                at = slice(2 * s, 2 * s + 2), slice(t * LANES, (t + 1) * LANES)
                ext_ref[var, plane + 2, t, EDGE - 2 : EDGE, :] = lo[(plane, *at)]
                ext_ref[var, plane + 2, t, EDGE + rows : EDGE + rows + 2, :] = hi[(plane, *at)]
        return carry

    @pl.when(group == 0)
    def _():
        for stage in stages:
            for c in stage:
                c.start()
        lax.fori_loop(0, planes, radial_layers, 0)
        for c in stages[0] + stages[1]:
            c.wait()

    def one(inner, carry):
        a = group * CHUNK + inner
        for i, stage in enumerate(stages[2:]):

            @pl.when(a == (i + 1) * CHUNK - 2)
            def _():
                for c in stage:
                    c.wait()

        half = 8
        for start in range(0, rows, half):
            at = slice(start, start + half)

            def part(var, offset, row_shift):
                first = EDGE + start + row_shift
                return [
                    ext_ref[var, a + 2 + offset, t, first : first + half, :] for t in range(tiles)
                ]

            held = [coef_ref[i, at, :] for i in range(coef_ref.shape[0])]

            def base(var):
                return [
                    base_ref[var, inner, at, t * LANES : (t + 1) * LANES] for t in range(tiles)
                ]

            totals = plane_update(part, held.__getitem__, base)
            for var in range(NVAR):
                for t in range(tiles):
                    next_ref[var, inner, at, t * LANES : (t + 1) * LANES] = totals[var][t]
        return carry

    lax.fori_loop(0, CHUNK, one, 0)


ANY = pl.BlockSpec(memory_space=pltpu.HBM)
IN_SMEM = pl.BlockSpec(memory_space=pltpu.SMEM)
IN_VMEM = pl.BlockSpec(memory_space=pltpu.VMEM)
MIB = 1 << 20


def limits(mib, **more):
    return pltpu.CompilerParams(vmem_limit_bytes=mib * MIB, **more)


def cost(flops, moved):
    return pl.CostEstimate(flops=flops, bytes_accessed=moved, transcendentals=0)


def in_hbm(array):
    return pltpu.with_memory_space_constraint(array, pltpu.HBM)


def whole(array):
    shape = array.shape
    return pl.BlockSpec(shape, lambda *_: (0,) * len(shape))


def pack_call(flow):
    nvar, planes, rows, length = flow.shape
    az_shape = jax.ShapeDtypeStruct((nvar, 2, rows, length), jnp.float32)
    rad_shape = jax.ShapeDtypeStruct((planes, 2 * len(FIRST_RAD), length), jnp.float32)
    shapes = (az_shape, az_shape, rad_shape, rad_shape)
    return pl.pallas_call(
        pack_kernel,
        name="pack",
        out_shape=shapes,
        in_specs=[ANY],
        out_specs=(IN_VMEM,) * len(shapes),
        scratch_shapes=[
            pltpu.VMEM((2, len(FIRST_RAD), planes, EDGE, length), jnp.float32),
            pltpu.SemaphoreType.DMA((2, len(FIRST_RAD))),
            pltpu.SemaphoreType.DMA((2,)),
        ],
        compiler_params=limits(8),
        cost_estimate=cost(0, 8 * nvar * 4 * rows * length),
    )(in_hbm(flow))


def panels_call(owner, count, line, mean_flow, order, flow, base, history):
    _, planes, rows, length = flow.shape
    owners, tiles = count.shape[1], length // LANES
    return pl.pallas_call(
        panels_kernel,
        name="panels",
        out_shape=(
            jax.ShapeDtypeStruct((owners, CAP * ROWS, LANES), jnp.bfloat16),
            jax.ShapeDtypeStruct((KMAX, 8, LANES), jnp.float32),
            jax.ShapeDtypeStruct((11, rows, LANES), jnp.float32),
            jax.ShapeDtypeStruct((1, order.shape[0]), jnp.float32),
            *[jax.ShapeDtypeStruct((planes, 2 * len(LATER_RAD), length), jnp.float32)] * 2,
            jax.ShapeDtypeStruct((LANES,), jnp.int32),
        ),
        in_specs=[ANY, IN_SMEM, IN_SMEM, IN_VMEM, IN_SMEM, ANY, ANY, IN_VMEM],
        out_specs=(IN_VMEM,) * 6 + (IN_SMEM,),
        scratch_shapes=[
            pltpu.VMEM((5, planes, tiles, rows, LANES), jnp.float32),
            pltpu.VMEM((ROWS, KMAX, LANES), jnp.float32),
            pltpu.VMEM((ROWS, LANES), jnp.float32),
            pltpu.VMEM((2, len(LATER_RAD), planes, EDGE, length), jnp.float32),
            pltpu.SMEM((owners,), jnp.int32),
            pltpu.SMEM(owner.shape[1:], jnp.int32),
            pltpu.SemaphoreType.DMA((6, tiles)),
            pltpu.SemaphoreType.DMA((2, len(LATER_RAD))),
        ],
        compiler_params=limits(10),
        cost_estimate=cost(0, 20 * MIB),
    )(in_hbm(owner), count, line, mean_flow, order, in_hbm(flow), in_hbm(base), history)


def fresh_call(slots, line, start, coef, rows, az, rad, held):
    length = az[0].shape[-1]
    band = az[0].shape[2]
    return pl.pallas_call(
        fresh_kernel,
        name="fresh",
        out_shape=jax.ShapeDtypeStruct(held.shape, held.dtype),
        in_specs=[IN_SMEM] * 3 + [IN_VMEM] * 2 + [pl.BlockSpec(memory_space=pl.ANY)] * 2 + [IN_VMEM] * 3,
        out_specs=IN_VMEM,
        scratch_shapes=[
            pltpu.VMEM((8, length // LANES, band, LANES), jnp.float32),
            pltpu.VMEM((8, LANES), jnp.float32),
            pltpu.SemaphoreType.DMA((2, 2, length // LANES)),
        ],
        compiler_params=limits(8),
        cost_estimate=cost(0, 4 * 4 * band * length * 4),
    )(slots, line, start, coef, rows, *az, *rad, held)


def fields_call(flow, az, base, rad0, rad1, coef):
    nvar, planes, rows, length = flow.shape
    cells = planes * rows * length
    every = (nvar, CHUNK, rows, length)
    args = (in_hbm(flow), *az, in_hbm(base), *rad0, *rad1, coef)
    return pl.pallas_call(
        fields_kernel,
        name="fields",
        out_shape=jax.ShapeDtypeStruct(flow.shape, jnp.float32),
        grid=(planes // CHUNK,),
        in_specs=[
            *[ANY] + [pl.BlockSpec(memory_space=pl.ANY)] * 2,
            pl.BlockSpec(every, lambda a: (0, a, 0, 0)),
            *[whole(x) for x in (*rad0, *rad1, coef)],
        ],
        out_specs=pl.BlockSpec(every, lambda a: (0, a, 0, 0)),
        scratch_shapes=[
            pltpu.VMEM(
                (nvar, planes + 4, length // LANES, rows + 2 * EDGE, LANES), jnp.float32
            ),
            pltpu.SemaphoreType.DMA((planes // CHUNK + 2, nvar, length // LANES)),
        ],
        compiler_params=limits(18, dimension_semantics=("arbitrary",)),
        cost_estimate=cost(250 * cells, 15 * 4 * cells),
    )(*args)


def weights_kernel(
    stations_ref,
    order_ref,
    weight_ref,
    out_ref,
    lhs_ref,
    held_ref,
    order_held_ref,
    spot_ref,
    sems,
):
    chunks, _, width = held_ref.shape
    copies = [
        pltpu.make_async_copy(
            weight_ref.at[:, pl.ds(i * width, width)], held_ref.at[i], sems.at[i]
        )
        for i in range(chunks)
    ]
    orders = pltpu.make_async_copy(order_ref, order_held_ref, sems.at[chunks])
    orders.start()
    for c in copies:
        c.start()
    for group in range(stations_ref.shape[0] * CAP // QUADS):
        tiles = []
        for m in range(QUADS):
            source, rank = divmod(group * QUADS + m, CAP)
            tile = stations_ref[source, rank * ROWS : (rank + 1) * ROWS, :]
            tiles.append(tile.astype(jnp.float32))
        for i, tile in enumerate(swap_quads(tiles)):
            lhs_ref[i * ROWS : (i + 1) * ROWS, group * LANES : (group + 1) * LANES] = tile.astype(
                lhs_ref.dtype
            )

    def place(j, carry):
        spot_ref[order_held_ref[j]] = j
        return carry

    orders.wait()
    lax.fori_loop(0, out_ref.shape[0], place, 0, unroll=8)
    groups = width // LANES
    for n, c in enumerate(copies):
        c.wait()
        part = jnp.dot(lhs_ref[...], held_ref[n], preferred_element_type=jnp.float32)
        for group in range(groups):
            lanes = slice(group * LANES, (group + 1) * LANES)
            tiles = [part[i * ROWS : (i + 1) * ROWS, lanes] for i in range(QUADS)]
            for m, tile in enumerate(swap_quads(tiles)):
                out_ref[spot_ref[(n * groups + group) * QUADS + m]] = tile


def weights_call(order, stations, weight):
    count = order.shape[0]
    depth, observers = weight.shape
    chunks = observers // WIDTH
    return pl.pallas_call(
        weights_kernel,
        name="observers",
        out_shape=jax.ShapeDtypeStruct((count, ROWS, LANES), jnp.float32),
        in_specs=[IN_VMEM, ANY, ANY],
        out_specs=IN_VMEM,
        scratch_shapes=[
            pltpu.VMEM((NT, depth), jnp.bfloat16),
            pltpu.VMEM((chunks, depth, WIDTH), jnp.bfloat16),
            pltpu.SMEM((count,), jnp.int32),
            pltpu.SMEM((count,), jnp.int32),
            pltpu.SemaphoreType.DMA((chunks + 1,)),
        ],
        compiler_params=limits(14),
        cost_estimate=cost(2 * NT * depth * observers, 2 * depth * observers),
    )(stations, in_hbm(order), in_hbm(weight))


def retard_kernel(total_ref, matrix_ref, out_ref, times_ref, late_ref):
    total = total_ref[...]
    for i in range(QUADS):
        turned = total if i == 0 else pltpu.roll(total, LANES - i * BP, 1)
        times_ref[pl.ds(i, ROWS, stride=QUADS), :] = turned
    late_ref[...] = jnp.dot(
        matrix_ref[...],
        times_ref[...],
        precision=lax.Precision.HIGHEST,
        preferred_element_type=jnp.float32,
    )
    lane = lax.broadcasted_iota(jnp.int32, (ROWS, LANES), 1)
    out = late_ref[pl.ds(0, ROWS, stride=QUADS), :]
    for i in range(1, QUADS):
        tile = pltpu.roll(late_ref[pl.ds(i, ROWS, stride=QUADS), :], i * BP, 1)
        out = jnp.where(lane >= i * BP, tile, out)
    out_ref[...] = out


def retard_call(total, matrix):
    return pl.pallas_call(
        retard_kernel,
        name="retard",
        out_shape=jax.ShapeDtypeStruct((ROWS, LANES), jnp.float32),
        in_specs=[pl.BlockSpec(memory_space=pltpu.VMEM)] * 2,
        out_specs=pl.BlockSpec(memory_space=pltpu.VMEM),
        scratch_shapes=[pltpu.VMEM((NT, LANES), jnp.float32)] * 2,
        compiler_params=limits(4),
        cost_estimate=cost(2 * NT * NT * LANES, 4 * NT * NT),
    )(total, matrix)


def exchange(first, last, axis, wrap):
    count = lax.axis_size(axis)
    up = [(i, (i + 1) % count) for i in range(count if wrap else count - 1)]
    down = [(j, i) for i, j in up]
    return lax.ppermute(last, axis, up), lax.ppermute(first, axis, down)


def per_device(
    flow_state,
    base_state,
    mean_flow,
    panel_history,
    panel_line,
    panel_start,
    panel_count,
    panel_owner,
    source_weight,
    retarded_time,
    observer_block,
):
    az_first, az_last, *ends = pack_call(flow_state)
    az = exchange(az_first, az_last, "azimuth", True)
    rad0 = exchange(*ends, "radius", False)
    history, local, coef, mask, *later, slots = panels_call(
        panel_owner,
        panel_count.T,
        panel_line,
        mean_flow,
        observer_block,
        flow_state,
        base_state,
        panel_history[0, 0],
    )
    outgoing = fresh_call(slots, panel_line, panel_start, coef, local, az, rad0, history)
    stations = lax.all_to_all(outgoing, "azimuth", split_axis=0, concat_axis=0, tiled=True)
    rad1 = exchange(*later, "radius", False)
    matrix = jnp.sum(retarded_time * mask[0][:, None, None], axis=0)
    sends = weights_call(observer_block, stations, source_weight[0])
    sends = (WIRE_SCALE * sends).astype(jnp.float16)
    parts = lax.all_to_all(sends, BOTH, split_axis=0, concat_axis=0, tiled=True)
    next_state = fields_call(flow_state, az, base_state, rad0, rad1, coef)

    total = (1.0 / WIRE_SCALE) * jnp.sum(parts.astype(jnp.float32), axis=0)
    pressure = retard_call(total, matrix)
    return next_state, pressure.reshape(1, ROWS * LANES)


def solution(mesh):
    placed = (
        P(None, "azimuth", "radius", None),
        P(None, "azimuth", "radius", None),
        P(None, "radius"),
        P("azimuth", "radius", None, None),
        P("azimuth", "radius", None),
        P("azimuth", "radius", None),
        P(),
        P(),
        P("radius", "azimuth", None),
        P(),
        P(),
    )

    return jax.shard_map(
        per_device,
        mesh=mesh,
        in_specs=placed,
        out_specs=(P(None, "azimuth", "radius", None), P(BOTH, None)),
        check_vma=False,
    )
```
